32 devices in a mesh: seq: 4 (over y, core), tp: 8 (over z, x).
Axes of the slice: x: 2, y: 2, z: 4, core: 2. Of those that a mesh axis runs over, the one named last changes fastest.
Arguments:
- tokens: bfloat16 [2048, 8192], P('seq', 'tp'), may hold values from -6 to 6
- w_query: bfloat16 [8192, 6144], P(None, 'tp'), may hold values from -0.0625 to 0.0625
- w_key: bfloat16 [8192, 6144], P(None, 'tp'), may hold values from -0.0625 to 0.0625
- w_value: bfloat16 [8192, 6144], P(None, 'tp'), may hold values from -0.0625 to 0.0625
- w_out: bfloat16 [6144, 8192], P('tp'), may hold values from -0.109375 to 0.109375
- carry: float32 [48, 128, 128], P('tp'), may hold values from -40 to 40
Outputs:
- mixed: bfloat16 [2048, 8192], P('seq', 'tp')
The draws below stay inside these ranges and needn't reach their ends.
All inputs are finite; a program needn't handle non-finite values.
Results may differ from the reference program's by a relative error of at most 0.0066.
Values may be sent and summed in bfloat16 or wider, within the bound.
No kernel may reach another device: no remote copies, remote signals or barrier semaphores. Data moves between devices by JAX's collectives and lax.ppermute only.
A program may use at most 192 MiB of HBM per device.

```python
import jax
import jax.numpy as jnp
from jax import lax

D = 8192
H = 48
HD = 128
TOK_DEV = 512
TOKENS = 2048
N_SEQ = 4


def strengthened(values, rng, source, target, shards_of, factor):
    owner, partner = [(jnp.arange(values.shape[dim]) // (values.shape[dim] // shards_of)).reshape([-1 if axis == dim else 1 for axis in range(values.ndim)]) for dim in (source, target)]
    chosen = jax.random.permutation(rng, shards_of)[partner]
    strong = (owner == chosen) | (owner == (partner + shards_of // 2) % shards_of)
    return jnp.where(strong, factor * values, values)


def levels(key, dims, split, low, largest):
    level = 1.0
    for dim, parts in split:
        heights = jax.random.uniform(jax.random.fold_in(jax.random.fold_in(key, 6), dim), (parts,), jnp.float32, low / len(split), largest / len(split))
        level = level * jnp.repeat(jnp.exp(heights), dims[dim] // parts).reshape((-1,) + (1,) * (len(dims) - 1 - dim))
    return level


def normal_values(rng, extent, scale, limit, cuts=(), kind=jnp.bfloat16):
    drawn = jax.random.normal(rng, extent, jnp.float32) * scale
    if len(cuts) > 0:
        drawn = levels(rng, extent, cuts, -0.22, 0.18) * drawn
    return jnp.clip(drawn, min=-limit, max=limit).astype(kind)


def bell_draw_with(key, shape, spread, bound, cuts, heavy, held_as=jnp.bfloat16):
    entries = spread * jax.random.normal(key, shape, jnp.float32)
    if cuts:
        entries = entries * levels(key, shape, cuts, -0.22, 0.18)
    return jnp.clip(strengthened(entries, jax.random.fold_in(key, 3), *heavy), -bound, bound).astype(held_as)


def setup_inputs(seed: int = 0) -> dict:
    key_of = jax.random.split(jax.random.key(seed), 7)
    return {
        "tokens": normal_values(key_of[0], (TOKENS, D), 1.0, 6.0, ((0, 4), (1, 8))),
        "w_query": normal_values(key_of[1], (D, H * HD), D ** -0.5, 0.0625, ((1, 8),)),
        "w_key": normal_values(key_of[2], (D, H * HD), D ** -0.5, 0.0625, ((1, 8),)),
        "w_value": normal_values(key_of[3], (D, H * HD), D ** -0.5, 0.0625, ((1, 8),)),
        "w_out": bell_draw_with(key_of[4], (H * HD, D), (H * HD) ** -0.5, 0.109375, ((0, 8),), (0, 1, 8, 2.0)),
        "carry": jnp.clip(jax.random.uniform(key_of[5], (H, HD, HD), jnp.float32, -40.0, 40.0) * levels(key_of[5], (H, HD, HD), ((0, 8),), -0.4, 0.0), -40.0, 40.0),
    }


EPSILON = 1e-05

def reference(tokens, w_query, w_key, w_value, w_out, carry):

    def project(weight):
        result = jnp.dot(tokens, weight, preferred_element_type=jnp.float32).astype(jnp.bfloat16)
        return result.reshape(N_SEQ, TOK_DEV, H, HD)
    query = project(w_query)
    keys_all = project(w_key)
    values_all = project(w_value)
    causal = jnp.arange(TOK_DEV)[:, None] >= jnp.arange(TOK_DEV)[None, :]

    def advance(state, blocks):
        query_block, key_block, value_block = blocks
        query_float = query_block.astype(jnp.float32)
        key_float = key_block.astype(jnp.float32)
        value_float = value_block.astype(jnp.float32)
        across = jnp.einsum('thd,hde->the', query_float, state, precision=lax.Precision.HIGHEST)
        scores = jnp.einsum('thd,shd->hts', query_float, key_float, precision=lax.Precision.HIGHEST)
        scores = jnp.where(causal[None], scores, 0.0).astype(jnp.bfloat16)
        scores = lax.optimization_barrier(scores).astype(jnp.float32)
        within = jnp.einsum('hts,she->the', scores, value_float, precision=lax.Precision.HIGHEST)
        total = across + within
        normed = total * lax.rsqrt(lax.optimization_barrier(jnp.mean(total * total, axis=-1, keepdims=True)) + EPSILON)
        state = state + jnp.einsum('thd,the->hde', key_float, value_float, precision=lax.Precision.HIGHEST)
        return (state, normed.astype(jnp.bfloat16))
    final_state, attended = lax.scan(advance, carry.astype(jnp.float32), (query, keys_all, values_all))
    attended = attended.reshape(TOKENS, H * HD)
    return jnp.dot(attended, w_out, preferred_element_type=jnp.float32).astype(jnp.bfloat16)
```

```python
import jax
import jax.numpy as jnp
from jax import lax
from jax.sharding import PartitionSpec as P

EPSILON = 1e-05
BF16 = jnp.bfloat16
F32 = jnp.float32


def ring_order(count):
    columns = 1
    while columns * columns * 4 <= count:
        columns *= 2
    rows = count // columns
    if rows % 2 or columns < 2:
        return list(range(count))
    order = [row * columns for row in range(rows)]
    for step, row in enumerate(reversed(range(rows))):
        span = range(1, columns) if step % 2 == 0 else range(columns - 1, 0, -1)
        order += [row * columns + column for column in span]
    return order


def dot(a, b):
    return jnp.dot(a, b, preferred_element_type=F32)


def prior_states(state, carry):
    count = lax.axis_size("seq")
    place = lax.axis_index("seq")
    partner = lax.ppermute(state, "seq", [(i, i ^ 1) for i in range(count)])
    total = state + partner
    prior = carry + jnp.where(place % 2 == 1, partner, 0.0)
    for shift in range(2, count, 2):
        prior = prior + lax.ppermute(total, "seq", [(i, i + shift) for i in range(count - shift)])
    return prior


def local(tokens, w_query, w_key, w_value, w_out, carry):
    row_count, chunk = tokens.shape
    head_count, head_size = carry.shape[:2]
    width = w_query.shape[1]
    half = row_count // 2
    count = lax.axis_size("tp")
    reach = count // 2
    order = ring_order(count)
    forward = [(order[i], order[(i + 1) % count]) for i in range(count)]
    backward = [(b, a) for a, b in forward]
    places = [order.index(i) for i in range(count)]
    place = jnp.asarray(places, jnp.int32)[lax.axis_index("tp")]

    def member(offset):
        return jnp.asarray(order, jnp.int32)[lax.rem(place + offset + count, count)]

    sums = [None, None, None]

    def take(block, owner):
        for i, weight in enumerate((w_query, w_key, w_value)):
            part = dot(block, lax.dynamic_slice_in_dim(weight, owner * chunk, chunk, 0))
            sums[i] = part if sums[i] is None else sums[i] + part

    ahead = [tokens[:half], tokens[half:]]
    behind = list(ahead)
    pending = [(tokens, member(0))]
    for step in range(1, reach + 1):
        ahead[0] = lax.ppermute(ahead[0], "tp", forward)
        behind[1] = lax.ppermute(behind[1], "tp", backward)
        if step < reach:
            ahead[1] = lax.ppermute(ahead[1], "tp", forward)
            behind[0] = lax.ppermute(behind[0], "tp", backward)
        for block, owner in pending:
            take(block, owner)
        if step < reach:
            pending = [
                (jnp.concatenate(ahead, 0), member(-step)),
                (jnp.concatenate(behind, 0), member(step)),
            ]
    take(jnp.concatenate([ahead[0], behind[1]], 0), member(reach))

    query, keys, values = [
        s.astype(BF16).reshape(row_count, head_count, head_size) for s in sums
    ]
    state = jnp.einsum("thd,the->hde", keys, values, preferred_element_type=F32)
    prior = prior_states(state, carry)
    prior_high = prior.astype(BF16)
    prior_low = (prior - prior_high.astype(F32)).astype(BF16)
    across = jnp.einsum("thd,hde->the", query, prior_high, preferred_element_type=F32)
    across = across + jnp.einsum("thd,hde->the", query, prior_low, preferred_element_type=F32)
    causal = lax.broadcasted_iota(jnp.int32, (row_count, row_count), 0) >= lax.broadcasted_iota(
        jnp.int32, (row_count, row_count), 1
    )
    scores = jnp.einsum("thd,shd->hts", query, keys, preferred_element_type=F32)
    scores = jnp.where(causal[None], scores, 0.0).astype(BF16)
    within = jnp.einsum("hts,she->the", scores, values, preferred_element_type=F32)
    total = across + within
    normed = total * lax.rsqrt(jnp.mean(total * total, axis=-1, keepdims=True) + EPSILON)
    attended = normed.astype(BF16).reshape(row_count, width)

    parts = (attended[:half], attended[half:])
    width_out = w_out.shape[1] // count

    def partial(rows, offset):
        columns = lax.dynamic_slice_in_dim(w_out, member(offset) * width_out, width_out, 1)
        return dot(parts[rows], columns)

    up = [None, None]
    down = [None, None]
    for distance in range(reach, 0, -1):
        for rows in (0, 1):
            if distance < reach or rows == 0:
                value = partial(rows, distance)
                if up[rows] is not None:
                    value = value + up[rows].astype(F32)
                up[rows] = lax.ppermute(value.astype(BF16), "tp", forward)
            if distance < reach or rows == 1:
                value = partial(rows, -distance)
                if down[rows] is not None:
                    value = value + down[rows].astype(F32)
                down[rows] = lax.ppermute(value.astype(BF16), "tp", backward)
    out = [
        (partial(rows, 0) + up[rows].astype(F32) + down[rows].astype(F32)).astype(BF16)
        for rows in (0, 1)
    ]
    return jnp.concatenate(out, 0)


def solution(mesh):
    placed = (
        P("seq", "tp"),
        P(None, "tp"),
        P(None, "tp"),
        P(None, "tp"),
        P("tp", None),
        P("tp", None, None),
    )
    return jax.shard_map(
        local, mesh=mesh, in_specs=placed, out_specs=P("seq", "tp"), check_vma=False
    )
```

```python
import functools

import jax
import jax.numpy as jnp
from jax import lax
from jax.experimental import pallas as pl
from jax.experimental.pallas import tpu as pltpu
from jax.sharding import PartitionSpec as P

EPSILON = 1e-05
BF16 = jnp.bfloat16
F32 = jnp.float32
PROJECT_BYTES = 34 << 20


def ring_order(count):
    columns = 1
    while columns * columns * 4 <= count:
        columns *= 2
    rows = count // columns
    if rows % 2 or columns < 2:
        return list(range(count))
    order = [row * columns for row in range(rows)]
    for step, row in enumerate(reversed(range(rows))):
        span = range(1, columns) if step % 2 == 0 else range(columns - 1, 0, -1)
        order += [row * columns + column for column in span]
    return order


def lookup(table, index):
    value = jnp.int32(table[0])
    for i, entry in enumerate(table[1:], 1):
        value = jnp.where(index == i, jnp.int32(entry), value)
    return value


def cut_at(array, start, size, axis):
    starts = [jnp.int32(0), jnp.int32(0)]
    sizes = list(array.shape)
    starts[axis], sizes[axis] = start, size
    return lax.dynamic_slice(array, starts, sizes, allow_negative_indices=False)


def dot(a, b):
    return jnp.dot(a, b, preferred_element_type=F32)


def dot_rows(a, b):
    return lax.dot_general(a, b, (((0,), (0,)), ((), ())), preferred_element_type=F32)


def dot_columns(a, b):
    return lax.dot_general(a, b, (((1,), (1,)), ((), ())), preferred_element_type=F32)


def kernel(body, inputs, outputs, aliases=None, scratch=(), vmem=16 << 20):
    return pl.pallas_call(
        body,
        in_specs=[pl.BlockSpec(memory_space=space) for _, space in inputs],
        out_specs=[pl.BlockSpec(memory_space=pltpu.VMEM) for _ in outputs],
        out_shape=[jax.ShapeDtypeStruct(shape, kind) for shape, kind in outputs],
        scratch_shapes=list(scratch),
        input_output_aliases=aliases or {},
        compiler_params=pltpu.CompilerParams(vmem_limit_bytes=vmem),
        cost_estimate=pl.CostEstimate(flops=0, bytes_accessed=1 << 20, transcendentals=0),
    )(*[array for array, _ in inputs])


def columns_of(j, block):
    return pl.ds(pl.multiple_of(j * block, block), block)


def project_body(pieces, has_sums, has_rows, block, place, next_place, has_columns, *refs):
    starts, xs, refs = refs[0], refs[1 : 1 + pieces], refs[1 + pieces :]
    weights, refs = refs[:3], refs[3:]
    if has_columns:
        (w_out, column_starts), refs = refs[:2], refs[2:]
    held, refs = (refs[:3], refs[3:]) if has_rows else (None, refs)
    sums, refs = (refs[:3], refs[3:]) if has_sums else (None, refs)
    outs, wanted, refs = refs[:3], refs[3:6], refs[6:]
    depth = xs[0].shape[1]

    def rows_to(k, targets, semaphores):
        rows = pl.ds(pl.multiple_of(starts[k], depth), depth)
        return [
            pltpu.make_async_copy(weights[i].at[rows, :], targets[i], semaphores.at[i])
            for i in range(3)
        ]

    brought = []
    if has_columns:
        target, refs = refs[0], refs[1:]
        size = target.shape[1]
        cut = pl.ds(pl.multiple_of(column_starts[next_place], size), size)
        brought.append(pltpu.make_async_copy(w_out.at[:, cut], target, refs[0].at[3]))
    brought = rows_to(next_place, wanted, refs[0]) + brought
    copies = []
    if not has_rows:
        held = refs[1:4]
        copies = rows_to(place, held, refs[4])
    for copy in (*copies, *brought):
        copy.start()
    chunk = jnp.concatenate([x[...] for x in xs], 0)
    for i in range(3):
        if copies:
            copies[i].wait()

        @pl.loop(0, outs[0].shape[1] // block)
        def _(j, i=i):
            cut = columns_of(j, block)
            part = dot(chunk, held[i][:, cut])
            outs[i][:, cut] = part if sums is None else sums[i][:, cut] + part

    for bring in brought:
        bring.wait()


def project(chunk, starts, place, weights, held, sums, block, next_place, extra=None):
    rows = sum(piece.shape[0] for piece in chunk)
    depth, width = chunk[0].shape[1], weights[0].shape[1]
    inputs = [(starts, pltpu.SMEM)] + [(array, pltpu.VMEM) for array in chunk]
    inputs += [(weight, pltpu.HBM) for weight in weights]
    outputs = [((rows, width), F32)] * 3 + [((depth, width), BF16)] * 3
    scratch = [pltpu.SemaphoreType.DMA((4,))]
    if extra is not None:
        w_out, column_starts, columns = extra
        inputs += [(w_out, pltpu.HBM), (column_starts, pltpu.SMEM)]
        outputs += [((w_out.shape[0], columns), BF16)]
    if held is None:
        scratch += [pltpu.VMEM((depth, width), BF16)] * 3 + [pltpu.SemaphoreType.DMA((3,))]
    else:
        inputs += [(weight, pltpu.VMEM) for weight in held]
    aliases = {}
    if sums is not None:
        aliases = {len(inputs) + i: i for i in range(3)}
        inputs += [(s, pltpu.VMEM) for s in sums]
    body = functools.partial(
        project_body,
        len(chunk),
        sums is not None,
        held is not None,
        block,
        place,
        next_place,
        extra is not None,
    )
    out = kernel(body, inputs, outputs, aliases, scratch, PROJECT_BYTES)
    return out[:3], out[3:]


def keys_body(pieces, size, block, *refs):
    xs = refs[:pieces]
    w_key, w_value, key_sum, value_sum, keys_out, values_out, state_out = refs[pieces:]
    heads = block // size
    chunk = jnp.concatenate([x[...] for x in xs], 0)

    @pl.loop(0, keys_out.shape[1] // block)
    def _(j):
        cut = columns_of(j, block)
        keys = (key_sum[:, cut] + dot(chunk, w_key[:, cut])).astype(BF16)
        keys_out[:, cut] = keys
        values = (value_sum[:, cut] + dot(chunk, w_value[:, cut])).astype(BF16)
        values_out[:, cut] = values
        for h in range(heads):
            own = slice(h * size, (h + 1) * size)
            state_out[j * heads + h] = dot_rows(keys[:, own], values[:, own])


def finish_keys(chunk, w_key, w_value, key_sum, value_sum, block, size):
    rows, width = key_sum.shape
    arrays = (*chunk, w_key, w_value, key_sum, value_sum)
    outputs = [((rows, width), BF16)] * 2 + [((width // size, size, size), F32)]
    body = functools.partial(keys_body, len(chunk), size, block)
    return kernel(body, [(array, pltpu.VMEM) for array in arrays], outputs)


def within_body(pieces, size, block, *refs):
    xs = refs[:pieces]
    w_query, query_sum, keys_in, values_in, query_out, within_out = refs[pieces:]
    rows, width = query_sum.shape
    chunk = jnp.concatenate([x[...] for x in xs], 0)
    tile = rows // 2
    causal = lax.broadcasted_iota(jnp.int32, (tile, tile), 0) >= lax.broadcasted_iota(
        jnp.int32, (tile, tile), 1
    )

    @pl.loop(0, width // block)
    def _(j):
        cut = columns_of(j, block)
        query = (query_sum[:, cut] + dot(chunk, w_query[:, cut])).astype(BF16)
        query_out[:, cut] = query
        keys, values = keys_in[:, cut], values_in[:, cut]
        sums = []
        for h in range(block // size):
            own = slice(h * size, (h + 1) * size)
            q, k, v = query[:, own], keys[:, own], values[:, own]
            first = jnp.where(causal, dot_columns(q[:tile], k[:tile]), 0.0).astype(BF16)
            lower = dot_columns(q[tile:], k[:tile]).astype(BF16)
            second = jnp.where(causal, dot_columns(q[tile:], k[tile:]), 0.0).astype(BF16)
            bottom = dot(lower, v[:tile]) + dot(second, v[tile:])
            sums.append(jnp.concatenate([dot(first, v[:tile]), bottom], 0))
        within_out[:, cut] = jnp.concatenate(sums, 1)


def finish_query(chunk, w_query, query_sum, keys, values, block, size):
    arrays = (*chunk, w_query, query_sum, keys, values)
    outputs = [(query_sum.shape, BF16), (query_sum.shape, F32)]
    body = functools.partial(within_body, len(chunk), size, block)
    return kernel(body, [(array, pltpu.VMEM) for array in arrays], outputs)


def attend_body(earlier, size, odd, query, within, carry, partner, *refs):
    others = refs[:earlier]
    w_first, top_out, bottom_out, top_first, bottom_first = refs[earlier:]
    heads = carry.shape[0]
    half = query.shape[0] // 2
    for h in range(heads):
        cut = slice(h * size, (h + 1) * size)
        prior = carry[h] + jnp.where(odd[0] == 1, partner[h], 0.0)
        for other in others:
            prior = prior + other[h].astype(F32)
        high = prior.astype(BF16)
        low = (prior - high.astype(F32)).astype(BF16)
        q = query[:, cut]
        o = within[:, cut] + dot(q, high) + dot(q, low)
        o = o * lax.rsqrt(jnp.mean(o * o, axis=-1, keepdims=True) + EPSILON)
        attended = o.astype(BF16)
        top_out[:, cut] = attended[:half]
        bottom_out[:, cut] = attended[half:]
    block = 256 if w_first.shape[1] % 256 == 0 else 128

    @pl.loop(0, w_first.shape[1] // block)
    def _(j):
        cut = columns_of(j, block)
        weight = w_first[:, cut]
        top_first[:, cut] = dot(top_out[...], weight).astype(BF16)
        bottom_first[:, cut] = dot(bottom_out[...], weight).astype(BF16)


def attend(odd, query, within, carry, partner, others, w_first, size):
    rows, width = query.shape
    inputs = [(odd, pltpu.SMEM)]
    inputs += [(s, pltpu.VMEM) for s in (query, within, carry, partner, *others, w_first)]
    outputs = [((rows // 2, width), BF16)] * 2 + [((rows // 2, w_first.shape[1]), BF16)] * 2
    return kernel(functools.partial(attend_body, len(others), size), inputs, outputs)


def pair_body(own, partner, out):
    out[...] = (own[...] + partner[...]).astype(BF16)


def finish_body(top_sum, bottom_sum, top, bottom, out):
    half = top.shape[0]
    out[:half] = (top_sum[...] + top[...].astype(F32)).astype(BF16)
    out[half:] = (bottom_sum[...] + bottom[...].astype(F32)).astype(BF16)


def local(tokens, w_query, w_key, w_value, w_out, carry):
    row_count = tokens.shape[0]
    head_count, size = carry.shape[:2]
    block = size * (2 if head_count % 2 == 0 else 1)
    half = row_count // 2
    count = lax.axis_size("tp")
    reach = count // 2
    order = ring_order(count)
    forward = [(order[i], order[(i + 1) % count]) for i in range(count)]
    backward = [(b, a) for a, b in forward]
    index = lax.axis_index("tp")
    depth = tokens.shape[1]
    columns = w_out.shape[1] // count

    offsets = list(range(-reach + 1, reach + 1))
    numbers = [
        lookup([order[(order.index(i) + offset) % count] for i in range(count)], index)
        for offset in offsets
    ]
    column_starts = [n * columns for n in numbers]
    row_table = jnp.stack([n * depth for n in numbers])
    column_table = jnp.stack(column_starts)
    odd = jnp.reshape(lax.rem(lax.axis_index("seq"), 2), (1,))
    tokens, odd, row_table, column_table, column_starts = lax.optimization_barrier(
        (tokens, odd, row_table, column_table, column_starts)
    )

    def add(chunk, offset, held, sums, next_offset, extra=None):
        places = offsets.index(offset), offsets.index(next_offset)
        return project(chunk, row_table, places[0], weights, held, sums, block, places[1], extra)

    weights = (w_query, w_key, w_value)
    offset_of = [0]
    for step in range(1, reach):
        offset_of += [-step, step]
    windows = 2 * reach - 1
    ahead = {(0, 0): tokens[:half], (0, 1): tokens[half:]}
    behind = dict(ahead)

    def send(slot):
        level, second = divmod(slot - 1, 2)
        up, down = (level, second), (level, 1 - second)
        ahead[level + 1, second] = lax.ppermute(ahead[up], "tp", forward)
        behind[level + 1, 1 - second] = lax.ppermute(behind[down], "tp", backward)

    def halves(offset):
        side = ahead if offset < 0 else behind
        return [side[abs(offset), 0], side[abs(offset), 1]]

    send(1)
    send(2)
    sums, held = add([tokens], 0, None, None, offset_of[1])
    for window in range(2, windows):
        level, second = divmod(window, 2)
        up, down = (level, second), (level, 1 - second)
        ahead[up], behind[down], sums, held = lax.optimization_barrier(
            (ahead[up], behind[down], sums, held)
        )
        send(window + 1)
        if window > 2:
            offset, following = offset_of[window - 2], offset_of[window - 1]
            sums, held = add(halves(offset), offset, held, sums, following)
    up, down = (reach - 1, 1), (reach - 1, 0)
    ahead[up], behind[down], sums, held = lax.optimization_barrier(
        (ahead[up], behind[down], sums, held)
    )
    offset, following = offset_of[-2:]
    sums, held = add(halves(offset), offset, held, sums, following)
    extra = (w_out, column_table, columns)
    sums, final = add(halves(following), following, held, sums, reach, extra)
    ahead, behind = ahead[reach, 0], behind[reach, 1]
    last = [ahead, behind]
    w_query_last, w_key_last, w_value_last, w_first = final
    keys, values, state = finish_keys(
        last, w_key_last, w_value_last, sums[1], sums[2], block, size
    )

    members = lax.axis_size("seq")
    partner = lax.ppermute(state, "seq", [(i, i ^ 1) for i in range(members)])
    pair = kernel(
        pair_body,
        [(state, pltpu.VMEM), (partner, pltpu.VMEM)],
        [(state.shape, BF16)],
    )[0]
    others = [
        lax.ppermute(pair, "seq", [(i, i + shift) for i in range(members - shift)])
        for shift in range(2, members, 2)
    ]
    query, within = finish_query(last, w_query_last, sums[0], keys, values, block, size)

    *parts, top, bottom = attend(odd, query, within, carry, partner, others, w_first, size)

    def partial(rows, offset):
        start = column_starts[offsets.index(offset)]
        return dot(parts[rows], cut_at(w_out, start, columns, 1))

    up = [lax.ppermute(top, "tp", forward), None]
    down = [None, lax.ppermute(bottom, "tp", backward)]
    for distance in range(reach - 1, 0, -1):
        for rows in (0, 1):
            for held, sign, hops in ((up, 1, forward), (down, -1, backward)):
                value = partial(rows, sign * distance)
                if held[rows] is not None:
                    value = value + held[rows].astype(F32)
                held[rows] = lax.ppermute(value.astype(BF16), "tp", hops)
    top_sum = partial(0, 0) + down[0].astype(F32)
    bottom_sum = partial(1, 0) + up[1].astype(F32)
    return kernel(
        finish_body,
        [(s, pltpu.VMEM) for s in (top_sum, bottom_sum, up[0], down[1])],
        [((row_count, columns), BF16)],
    )[0]


def solution(mesh):
    placed = (
        P("seq", "tp"),
        P(None, "tp"),
        P(None, "tp"),
        P(None, "tp"),
        P("tp", None),
        P("tp", None, None),
    )
    return jax.shard_map(
        local, mesh=mesh, in_specs=placed, out_specs=P("seq", "tp"), check_vma=False
    )
```

```python
import functools

import jax
import jax.numpy as jnp
from jax import lax
from jax.experimental import pallas as pl
from jax.experimental.pallas import tpu as pltpu
from jax.sharding import PartitionSpec as P

EPSILON = 1e-05
BF16 = jnp.bfloat16
F32 = jnp.float32
PROJECT_BYTES = 34 << 20


def ring_order(count):
    columns = 1
    while columns * columns * 4 <= count:
        columns *= 2
    rows = count // columns
    if rows % 2 or columns < 2:
        return list(range(count))
    order = [row * columns for row in range(rows)]
    for step, row in enumerate(reversed(range(rows))):
        span = range(1, columns) if step % 2 == 0 else range(columns - 1, 0, -1)
        order += [row * columns + column for column in span]
    return order


def lookup(table, index):
    value = jnp.int32(table[0])
    for i, entry in enumerate(table[1:], 1):
        value = jnp.where(index == i, jnp.int32(entry), value)
    return value


def cut_at(array, start, size, axis):
    starts = [jnp.int32(0), jnp.int32(0)]
    sizes = list(array.shape)
    starts[axis], sizes[axis] = start, size
    return lax.dynamic_slice(array, starts, sizes, allow_negative_indices=False)


def dot(a, b):
    return jnp.dot(a, b, preferred_element_type=F32)


def dot_rows(a, b):
    return lax.dot_general(a, b, (((0,), (0,)), ((), ())), preferred_element_type=F32)


def dot_columns(a, b):
    return lax.dot_general(a, b, (((1,), (1,)), ((), ())), preferred_element_type=F32)


def kernel(body, inputs, outputs, aliases=None, scratch=(), vmem=16 << 20):
    return pl.pallas_call(
        body,
        in_specs=[pl.BlockSpec(memory_space=space) for _, space in inputs],
        out_specs=[pl.BlockSpec(memory_space=pltpu.VMEM) for _ in outputs],
        out_shape=[jax.ShapeDtypeStruct(shape, kind) for shape, kind in outputs],
        scratch_shapes=list(scratch),
        input_output_aliases=aliases or {},
        compiler_params=pltpu.CompilerParams(vmem_limit_bytes=vmem),
        cost_estimate=pl.CostEstimate(flops=0, bytes_accessed=1 << 20, transcendentals=0),
    )(*[array for array, _ in inputs])


def columns_of(j, block):
    return pl.ds(pl.multiple_of(j * block, block), block)


def project_body(pieces, has_sums, has_rows, block, place, next_place, has_columns, *refs):
    starts, xs, refs = refs[0], refs[1 : 1 + pieces], refs[1 + pieces :]
    weights, refs = refs[:3], refs[3:]
    if has_columns:
        (w_out, column_starts), refs = refs[:2], refs[2:]
    held, refs = (refs[:3], refs[3:]) if has_rows else (None, refs)
    sums, refs = (refs[:3], refs[3:]) if has_sums else (None, refs)
    outs, wanted, refs = refs[:3], refs[3:6], refs[6:]
    depth = xs[0].shape[1]

    def rows_to(k, targets, semaphores):
        rows = pl.ds(pl.multiple_of(starts[k], depth), depth)
        return [
            pltpu.make_async_copy(weights[i].at[rows, :], targets[i], semaphores.at[i])
            for i in range(3)
        ]

    brought = []
    if has_columns:
        target, refs = refs[0], refs[1:]
        size = target.shape[1]
        cut = pl.ds(pl.multiple_of(column_starts[next_place], size), size)
        brought.append(pltpu.make_async_copy(w_out.at[:, cut], target, refs[0].at[3]))
    brought = rows_to(next_place, wanted, refs[0]) + brought
    copies = []
    if not has_rows:
        held = refs[1:4]
        copies = rows_to(place, held, refs[4])
    for copy in (*copies, *brought):
        copy.start()
    chunk = jnp.concatenate([x[...] for x in xs], 0)
    for i in range(3):
        if copies:
            copies[i].wait()

        @pl.loop(0, outs[0].shape[1] // block)
        def _(j, i=i):
            cut = columns_of(j, block)
            part = dot(chunk, held[i][:, cut])
            outs[i][:, cut] = part if sums is None else sums[i][:, cut] + part

    for bring in brought:
        bring.wait()


def project(chunk, starts, place, weights, held, sums, block, next_place, extra=None):
    rows = sum(piece.shape[0] for piece in chunk)
    depth, width = chunk[0].shape[1], weights[0].shape[1]
    inputs = [(starts, pltpu.SMEM)] + [(array, pltpu.VMEM) for array in chunk]
    inputs += [(weight, pltpu.HBM) for weight in weights]
    outputs = [((rows, width), F32)] * 3 + [((depth, width), BF16)] * 3
    scratch = [pltpu.SemaphoreType.DMA((4,))]
    if extra is not None:
        w_out, column_starts, columns = extra
        inputs += [(w_out, pltpu.HBM), (column_starts, pltpu.SMEM)]
        outputs += [((w_out.shape[0], columns), BF16)]
    if held is None:
        scratch += [pltpu.VMEM((depth, width), BF16)] * 3 + [pltpu.SemaphoreType.DMA((3,))]
    else:
        inputs += [(weight, pltpu.VMEM) for weight in held]
    aliases = {}
    if sums is not None:
        aliases = {len(inputs) + i: i for i in range(3)}
        inputs += [(s, pltpu.VMEM) for s in sums]
    body = functools.partial(
        project_body,
        len(chunk),
        sums is not None,
        held is not None,
        block,
        place,
        next_place,
        extra is not None,
    )
    out = kernel(body, inputs, outputs, aliases, scratch, PROJECT_BYTES)
    return out[:3], out[3:]


def keys_body(pieces, size, block, *refs):
    xs = refs[:pieces]
    w_key, w_value, key_sum, value_sum, keys_out, values_out, state_out, sent_out = refs[pieces:]
    heads = block // size
    chunk = jnp.concatenate([x[...] for x in xs], 0)
    for j in range(keys_out.shape[1] // block):
        cut = slice(j * block, (j + 1) * block)
        keys = (key_sum[:, cut] + dot(chunk, w_key[:, cut])).astype(BF16)
        keys_out[:, cut] = keys
        values = (value_sum[:, cut] + dot(chunk, w_value[:, cut])).astype(BF16)
        values_out[:, cut] = values
        states = dot_rows(keys, values)
        for h in range(heads):
            own = slice(h * size, (h + 1) * size)
            state_out[j * heads + h] = states[own, own]
            sent_out[j * heads + h] = states[own, own].astype(BF16)


def finish_keys(chunk, w_key, w_value, key_sum, value_sum, block, size):
    rows, width = key_sum.shape
    arrays = (*chunk, w_key, w_value, key_sum, value_sum)
    outputs = [((rows, width), BF16)] * 2
    outputs += [((width // size, size, size), kind) for kind in (F32, BF16)]
    body = functools.partial(keys_body, len(chunk), size, block)
    return kernel(body, [(array, pltpu.VMEM) for array in arrays], outputs)


def within_body(pieces, size, block, *refs):
    xs = refs[:pieces]
    w_query, query_sum, keys_in, values_in, query_out, within_out = refs[pieces:]
    rows, width = query_sum.shape
    chunk = jnp.concatenate([x[...] for x in xs], 0)
    tile = rows // 2
    causal = lax.broadcasted_iota(jnp.int32, (tile, tile), 0) >= lax.broadcasted_iota(
        jnp.int32, (tile, tile), 1
    )

    @pl.loop(0, width // block)
    def _(j):
        cut = columns_of(j, block)
        query = (query_sum[:, cut] + dot(chunk, w_query[:, cut])).astype(BF16)
        query_out[:, cut] = query
        keys, values = keys_in[:, cut], values_in[:, cut]
        sums = []
        for h in range(block // size):
            own = slice(h * size, (h + 1) * size)
            q, k, v = query[:, own], keys[:, own], values[:, own]
            first = jnp.where(causal, dot_columns(q[:tile], k[:tile]), 0.0).astype(BF16)
            lower = dot_columns(q[tile:], k[:tile]).astype(BF16)
            second = jnp.where(causal, dot_columns(q[tile:], k[tile:]), 0.0).astype(BF16)
            bottom = dot(lower, v[:tile]) + dot(second, v[tile:])
            sums.append(jnp.concatenate([dot(first, v[:tile]), bottom], 0))
        within_out[:, cut] = jnp.concatenate(sums, 1)


def finish_query(chunk, w_query, query_sum, keys, values, block, size):
    arrays = (*chunk, w_query, query_sum, keys, values)
    outputs = [(query_sum.shape, BF16), (query_sum.shape, F32)]
    body = functools.partial(within_body, len(chunk), size, block)
    return kernel(body, [(array, pltpu.VMEM) for array in arrays], outputs)


def attend_body(earlier, size, odd, query, within, carry, partner, *refs):
    others = refs[:earlier]
    w_first, top_out, bottom_out, top_first, bottom_first = refs[earlier:]
    heads = carry.shape[0]
    half = query.shape[0] // 2
    for h in range(heads):
        cut = slice(h * size, (h + 1) * size)
        prior = carry[h] + jnp.where(odd[0] == 1, partner[h].astype(F32), 0.0)
        for other in others:
            prior = prior + other[h].astype(F32)
        high = prior.astype(BF16)
        low = (prior - high.astype(F32)).astype(BF16)
        q = query[:, cut]
        o = within[:, cut] + dot(jnp.concatenate([q, q], 1), jnp.concatenate([high, low], 0))
        o = o * lax.rsqrt(jnp.mean(o * o, axis=-1, keepdims=True) + EPSILON)
        attended = o.astype(BF16)
        top_out[:, cut] = attended[:half]
        bottom_out[:, cut] = attended[half:]
    block = 256 if w_first.shape[1] % 256 == 0 else 128

    for j in range(w_first.shape[1] // block):
        cut = slice(j * block, (j + 1) * block)
        weight = w_first[:, cut]
        top_first[:, cut] = dot(top_out[...], weight).astype(BF16)
        bottom_first[:, cut] = dot(bottom_out[...], weight).astype(BF16)


def attend(odd, query, within, carry, partner, others, w_first, size):
    rows, width = query.shape
    inputs = [(odd, pltpu.SMEM)]
    inputs += [(s, pltpu.VMEM) for s in (query, within, carry, partner, *others, w_first)]
    outputs = [((rows // 2, width), BF16)] * 2 + [((rows // 2, w_first.shape[1]), BF16)] * 2
    return kernel(functools.partial(attend_body, len(others), size), inputs, outputs)


def pair_body(own, partner, out):
    out[...] = (own[...] + partner[...].astype(F32)).astype(BF16)


def finish_body(top_sum, bottom_sum, top, bottom, out, staged, moved):
    half = top.shape[0]
    copies = []
    for i, (total, last) in enumerate(((top_sum, top), (bottom_sum, bottom))):
        cut = slice(i * half, (i + 1) * half)
        staged[cut] = (total[...] + last[...].astype(F32)).astype(BF16)
        copies.append(pltpu.make_async_copy(staged.at[cut, :], out.at[cut, :], moved.at[i]))
        copies[-1].start()
    for copy in copies:
        copy.wait()


def finish(arrays):
    shape = (2 * arrays[0].shape[0], arrays[0].shape[1])
    return pl.pallas_call(
        finish_body,
        in_specs=[pl.BlockSpec(memory_space=pltpu.VMEM)] * 4,
        out_specs=pl.BlockSpec(memory_space=pltpu.HBM),
        out_shape=jax.ShapeDtypeStruct(shape, BF16),
        scratch_shapes=[pltpu.VMEM(shape, BF16), pltpu.SemaphoreType.DMA((2,))],
        compiler_params=pltpu.CompilerParams(vmem_limit_bytes=16 << 20),
        cost_estimate=pl.CostEstimate(flops=0, bytes_accessed=1 << 20, transcendentals=0),
    )(*arrays)


def local(tokens, w_query, w_key, w_value, w_out, carry):
    row_count = tokens.shape[0]
    head_count, size = carry.shape[:2]
    block = size * (2 if head_count % 2 == 0 else 1)
    half = row_count // 2
    count = lax.axis_size("tp")
    reach = count // 2
    order = ring_order(count)
    forward = [(order[i], order[(i + 1) % count]) for i in range(count)]
    backward = [(b, a) for a, b in forward]
    index = lax.axis_index("tp")
    depth = tokens.shape[1]
    columns = w_out.shape[1] // count

    offsets = list(range(-reach + 1, reach + 1))
    numbers = [
        lookup([order[(order.index(i) + offset) % count] for i in range(count)], index)
        for offset in offsets
    ]
    column_starts = [n * columns for n in numbers]
    row_table = jnp.stack([n * depth for n in numbers])
    column_table = jnp.stack(column_starts)
    odd = jnp.reshape(lax.rem(lax.axis_index("seq"), 2), (1,))
    tokens, odd, row_table, column_table, column_starts = lax.optimization_barrier(
        (tokens, odd, row_table, column_table, column_starts)
    )

    def add(chunk, offset, held, sums, next_offset, extra=None):
        places = offsets.index(offset), offsets.index(next_offset)
        return project(chunk, row_table, places[0], weights, held, sums, block, places[1], extra)

    weights = (w_query, w_key, w_value)
    offset_of = [0]
    for step in range(1, reach):
        offset_of += [-step, step]
    windows = 2 * reach - 1
    ahead = {(0, 0): tokens[:half], (0, 1): tokens[half:]}
    behind = dict(ahead)

    def send(slot):
        level, second = divmod(slot - 1, 2)
        up, down = (level, second), (level, 1 - second)
        ahead[level + 1, second] = lax.ppermute(ahead[up], "tp", forward)
        behind[level + 1, 1 - second] = lax.ppermute(behind[down], "tp", backward)

    def halves(offset):
        side = ahead if offset < 0 else behind
        return [side[abs(offset), 0], side[abs(offset), 1]]

    send(1)
    send(2)
    sums, held = add([tokens], 0, None, None, offset_of[1])
    for window in range(2, windows):
        level, second = divmod(window, 2)
        up, down = (level, second), (level, 1 - second)
        ahead[up], behind[down], sums, held = lax.optimization_barrier(
            (ahead[up], behind[down], sums, held)
        )
        send(window + 1)
        if window > 2:
            offset, following = offset_of[window - 2], offset_of[window - 1]
            sums, held = add(halves(offset), offset, held, sums, following)
    up, down = (reach - 1, 1), (reach - 1, 0)
    ahead[up], behind[down], sums, held = lax.optimization_barrier(
        (ahead[up], behind[down], sums, held)
    )
    offset, following = offset_of[-2:]
    sums, held = add(halves(offset), offset, held, sums, following)
    extra = (w_out, column_table, columns)
    sums, final = add(halves(following), following, held, sums, reach, extra)
    ahead, behind = ahead[reach, 0], behind[reach, 1]
    last = [ahead, behind]
    w_query_last, w_key_last, w_value_last, w_first = final
    keys, values, state, sent = finish_keys(
        last, w_key_last, w_value_last, sums[1], sums[2], block, size
    )

    members = lax.axis_size("seq")
    partner = lax.ppermute(sent, "seq", [(i, i ^ 1) for i in range(members)])
    pair = kernel(
        pair_body,
        [(state, pltpu.VMEM), (partner, pltpu.VMEM)],
        [(state.shape, BF16)],
    )[0]
    others = [
        lax.ppermute(pair, "seq", [(i, i + shift) for i in range(members - shift)])
        for shift in range(2, members, 2)
    ]
    query, within = finish_query(last, w_query_last, sums[0], keys, values, block, size)

    *parts, top, bottom = attend(odd, query, within, carry, partner, others, w_first, size)

    def partial(rows, offset):
        start = column_starts[offsets.index(offset)]
        return dot(parts[rows], cut_at(w_out, start, columns, 1))

    up = [lax.ppermute(top, "tp", forward), None]
    down = [None, lax.ppermute(bottom, "tp", backward)]
    for distance in range(reach - 1, 0, -1):
        for rows in (0, 1):
            for held, sign, hops in ((up, 1, forward), (down, -1, backward)):
                value = partial(rows, sign * distance)
                if held[rows] is not None:
                    value = value + held[rows].astype(F32)
                held[rows] = lax.ppermute(value.astype(BF16), "tp", hops)
    top_sum = partial(0, 0) + down[0].astype(F32)
    bottom_sum = partial(1, 0) + up[1].astype(F32)
    return finish((top_sum, bottom_sum, up[0], down[1]))


def solution(mesh):
    placed = (
        P("seq", "tp"),
        P(None, "tp"),
        P(None, "tp"),
        P(None, "tp"),
        P("tp", None),
        P("tp", None, None),
    )
    return jax.shard_map(
        local, mesh=mesh, in_specs=placed, out_specs=P("seq", "tp"), check_vma=False
    )
```

```python
import functools

import jax
import jax.numpy as jnp
from jax import lax
from jax.experimental import pallas as pl
from jax.experimental.pallas import tpu as pltpu
from jax.sharding import PartitionSpec as P

EPSILON = 1e-05
BF16 = jnp.bfloat16
F32 = jnp.float32
PROJECT_BYTES = 32 << 20


def ring_order(count):
    columns = 1
    while columns * columns * 4 <= count:
        columns *= 2
    rows = count // columns
    if rows % 2 or columns < 2:
        return list(range(count))
    order = [row * columns for row in range(rows)]
    for step, row in enumerate(reversed(range(rows))):
        span = range(1, columns) if step % 2 == 0 else range(columns - 1, 0, -1)
        order += [row * columns + column for column in span]
    return order


def lookup(table, index):
    value = jnp.int32(table[0])
    for i, entry in enumerate(table[1:], 1):
        value = jnp.where(index == i, jnp.int32(entry), value)
    return value


def cut_at(array, start, size, axis):
    starts = [jnp.int32(0), jnp.int32(0)]
    sizes = list(array.shape)
    starts[axis], sizes[axis] = start, size
    return lax.dynamic_slice(array, starts, sizes, allow_negative_indices=False)


def dot(a, b):
    return jnp.dot(a, b, preferred_element_type=F32)


def dot_rows(a, b):
    return lax.dot_general(a, b, (((0,), (0,)), ((), ())), preferred_element_type=F32)


def dot_columns(a, b):
    return lax.dot_general(a, b, (((1,), (1,)), ((), ())), preferred_element_type=F32)


def kernel(body, inputs, outputs, aliases=None, scratch=(), vmem=16 << 20):
    return pl.pallas_call(
        body,
        in_specs=[pl.BlockSpec(memory_space=space) for _, space in inputs],
        out_specs=[pl.BlockSpec(memory_space=pltpu.VMEM) for _ in outputs],
        out_shape=[jax.ShapeDtypeStruct(shape, kind) for shape, kind in outputs],
        scratch_shapes=list(scratch),
        input_output_aliases=aliases or {},
        compiler_params=pltpu.CompilerParams(vmem_limit_bytes=vmem),
        cost_estimate=pl.CostEstimate(flops=0, bytes_accessed=1 << 20, transcendentals=0),
    )(*[array for array, _ in inputs])


def columns_of(j, block):
    return pl.ds(pl.multiple_of(j * block, block), block)


def project_body(pieces, has_sums, has_rows, block, place, bring, has_columns, *refs):
    starts, xs, refs = refs[0], refs[1 : 1 + pieces], refs[1 + pieces :]
    weights, refs = refs[:3], refs[3:]
    if has_columns:
        (w_out, column_starts), refs = refs[:2], refs[2:]
    held, refs = (refs[:3], refs[3:]) if has_rows else (None, refs)
    sums, refs = (refs[:3], refs[3:]) if has_sums else (None, refs)
    outs, refs = refs[:3], refs[3:]
    wanted, refs = refs[: 3 * len(bring)], refs[3 * len(bring) :]
    depth = xs[0].shape[1]

    def rows_to(k, targets, semaphores, first=0):
        rows = pl.ds(pl.multiple_of(starts[k], depth), depth)
        return [
            pltpu.make_async_copy(weights[i].at[rows, :], targets[i], semaphores.at[first + i])
            for i in range(3)
        ]

    if has_columns:
        target, refs = refs[0], refs[1:]
    brought = []
    for n, k in enumerate(bring):
        brought += rows_to(k, wanted[3 * n : 3 * n + 3], refs[0], 3 * n)
    if has_columns:
        size = target.shape[1]
        cut = pl.ds(pl.multiple_of(column_starts[bring[0]], size), size)
        brought.append(pltpu.make_async_copy(w_out.at[:, cut], target, refs[0].at[3 * len(bring)]))
    copies = []
    if not has_rows:
        held = refs[1:4]
        copies = rows_to(place, held, refs[4])
    for copy in (*copies, *brought):
        copy.start()
    chunk = jnp.concatenate([x[...] for x in xs], 0)
    for copy in copies:
        copy.wait()

    @pl.loop(0, outs[0].shape[1] // block)
    def _(j):
        cut = columns_of(j, block)
        for i in range(3):
            part = dot(chunk, held[i][:, cut])
            outs[i][:, cut] = part if sums is None else sums[i][:, cut] + part

    for copy in brought:
        copy.wait()


def project(chunk, starts, place, weights, held, sums, block, bring, extra=None):
    rows = sum(piece.shape[0] for piece in chunk)
    depth, width = chunk[0].shape[1], weights[0].shape[1]
    inputs = [(starts, pltpu.SMEM)] + [(array, pltpu.VMEM) for array in chunk]
    inputs += [(weight, pltpu.HBM) for weight in weights]
    outputs = [((rows, width), F32)] * 3 + [((depth, width), BF16)] * (3 * len(bring))
    scratch = [pltpu.SemaphoreType.DMA((3 * len(bring) + 1,))]
    if extra is not None:
        w_out, column_starts, columns = extra
        inputs += [(w_out, pltpu.HBM), (column_starts, pltpu.SMEM)]
        outputs += [((w_out.shape[0], columns), BF16)]
    if held is None:
        scratch += [pltpu.VMEM((depth, width), BF16)] * 3 + [pltpu.SemaphoreType.DMA((3,))]
    else:
        inputs += [(weight, pltpu.VMEM) for weight in held]
    aliases = {}
    if sums is not None:
        aliases = {len(inputs) + i: i for i in range(3)}
        inputs += [(s, pltpu.VMEM) for s in sums]
    body = functools.partial(
        project_body,
        len(chunk),
        sums is not None,
        held is not None,
        block,
        place,
        bring,
        extra is not None,
    )
    out = kernel(body, inputs, outputs, aliases, scratch, PROJECT_BYTES)
    sets = [out[3 + 3 * n : 6 + 3 * n] for n in range(len(bring))]
    return out[:3], sets, out[3 + 3 * len(bring) :]


def keys_body(pieces, size, block, *refs):
    xs = refs[:pieces]
    w_key, w_value, key_sum, value_sum, keys_out, values_out, state_out, sent_out = refs[pieces:]
    heads = block // size
    chunk = jnp.concatenate([x[...] for x in xs], 0)
    for j in range(keys_out.shape[1] // block):
        cut = slice(j * block, (j + 1) * block)
        keys = (key_sum[:, cut] + dot(chunk, w_key[:, cut])).astype(BF16)
        keys_out[:, cut] = keys
        values = (value_sum[:, cut] + dot(chunk, w_value[:, cut])).astype(BF16)
        values_out[:, cut] = values
        states = dot_rows(keys, values)
        for h in range(heads):
            own = slice(h * size, (h + 1) * size)
            state_out[j * heads + h] = states[own, own]
            sent_out[j * heads + h] = states[own, own].astype(BF16)


def finish_keys(chunk, w_key, w_value, key_sum, value_sum, block, size):
    rows, width = key_sum.shape
    arrays = (*chunk, w_key, w_value, key_sum, value_sum)
    outputs = [((rows, width), BF16)] * 2
    outputs += [((width // size, size, size), kind) for kind in (F32, BF16)]
    body = functools.partial(keys_body, len(chunk), size, block)
    return kernel(body, [(array, pltpu.VMEM) for array in arrays], outputs)


def within_body(pieces, size, block, *refs):
    xs = refs[:pieces]
    w_query, query_sum, keys_in, values_in, query_out, within_out = refs[pieces:]
    rows, width = query_sum.shape
    chunk = jnp.concatenate([x[...] for x in xs], 0)
    tile = rows // 2
    causal = lax.broadcasted_iota(jnp.int32, (tile, tile), 0) >= lax.broadcasted_iota(
        jnp.int32, (tile, tile), 1
    )

    for j in range(width // block):
        cut = slice(j * block, (j + 1) * block)
        query = (query_sum[:, cut] + dot(chunk, w_query[:, cut])).astype(BF16)
        query_out[:, cut] = query
        keys, values = keys_in[:, cut], values_in[:, cut]
        sums = []
        for h in range(block // size):
            own = slice(h * size, (h + 1) * size)
            q, k, v = query[:, own], keys[:, own], values[:, own]
            first = jnp.where(causal, dot_columns(q[:tile], k[:tile]), 0.0).astype(BF16)
            lower = dot_columns(q[tile:], k[:tile]).astype(BF16)
            second = jnp.where(causal, dot_columns(q[tile:], k[tile:]), 0.0).astype(BF16)
            bottom = dot(lower, v[:tile]) + dot(second, v[tile:])
            sums.append(jnp.concatenate([dot(first, v[:tile]), bottom], 0))
        within_out[:, cut] = jnp.concatenate(sums, 1)


def finish_query(chunk, w_query, query_sum, keys, values, block, size):
    arrays = (*chunk, w_query, query_sum, keys, values)
    outputs = [(query_sum.shape, BF16), (query_sum.shape, F32)]
    body = functools.partial(within_body, len(chunk), size, block)
    return kernel(body, [(array, pltpu.VMEM) for array in arrays], outputs)


def attend_body(earlier, size, query, within, carry, *refs):
    others = refs[:earlier]
    w_first, top_out, bottom_out, top_first, bottom_first = refs[earlier:]
    heads = carry.shape[0]
    half = query.shape[0] // 2
    for h in range(heads):
        cut = slice(h * size, (h + 1) * size)
        prior = carry[h]
        for other in others:
            prior = prior + other[h].astype(F32)
        high = prior.astype(BF16)
        low = (prior - high.astype(F32)).astype(BF16)
        q = query[:, cut]
        o = within[:, cut] + dot(jnp.concatenate([q, q], 1), jnp.concatenate([high, low], 0))
        o = o * lax.rsqrt(jnp.mean(o * o, axis=-1, keepdims=True) + EPSILON)
        attended = o.astype(BF16)
        top_out[:, cut] = attended[:half]
        bottom_out[:, cut] = attended[half:]
    block = 256 if w_first.shape[1] % 256 == 0 else 128

    for j in range(w_first.shape[1] // block):
        cut = slice(j * block, (j + 1) * block)
        weight = w_first[:, cut]
        top_first[:, cut] = dot(top_out[...], weight).astype(BF16)
        bottom_first[:, cut] = dot(bottom_out[...], weight).astype(BF16)


def attend(query, within, carry, others, w_first, size):
    rows, width = query.shape
    inputs = [(s, pltpu.VMEM) for s in (query, within, carry, *others, w_first)]
    outputs = [((rows // 2, width), BF16)] * 2 + [((rows // 2, w_first.shape[1]), BF16)] * 2
    return kernel(functools.partial(attend_body, len(others), size), inputs, outputs)


def share_body(odd, own, *refs):
    *others, out = refs
    total = jnp.where(odd[0] == 1, 0.0, own[...])
    for other in others:
        total = total + other[...].astype(F32)
    out[...] = total.astype(BF16)


def finish_body(top_sum, bottom_sum, top, bottom, out, staged, moved):
    half = top.shape[0]
    copies = []
    for i, (total, last) in enumerate(((top_sum, top), (bottom_sum, bottom))):
        cut = slice(i * half, (i + 1) * half)
        staged[cut] = (total[...] + last[...].astype(F32)).astype(BF16)
        copies.append(pltpu.make_async_copy(staged.at[cut, :], out.at[cut, :], moved.at[i]))
        copies[-1].start()
    for copy in copies:
        copy.wait()


def finish(arrays):
    shape = (2 * arrays[0].shape[0], arrays[0].shape[1])
    return pl.pallas_call(
        finish_body,
        in_specs=[pl.BlockSpec(memory_space=pltpu.VMEM)] * 4,
        out_specs=pl.BlockSpec(memory_space=pltpu.HBM),
        out_shape=jax.ShapeDtypeStruct(shape, BF16),
        scratch_shapes=[pltpu.VMEM(shape, BF16), pltpu.SemaphoreType.DMA((2,))],
        compiler_params=pltpu.CompilerParams(vmem_limit_bytes=16 << 20),
        cost_estimate=pl.CostEstimate(flops=0, bytes_accessed=1 << 20, transcendentals=0),
    )(*arrays)


def local(tokens, w_query, w_key, w_value, w_out, carry):
    row_count = tokens.shape[0]
    head_count, size = carry.shape[:2]
    block = size * (2 if head_count % 2 == 0 else 1)
    half = row_count // 2
    count = lax.axis_size("tp")
    reach = count // 2
    order = ring_order(count)
    forward = [(order[i], order[(i + 1) % count]) for i in range(count)]
    backward = [(b, a) for a, b in forward]
    index = lax.axis_index("tp")
    depth = tokens.shape[1]
    columns = w_out.shape[1] // count

    offsets = list(range(-reach + 1, reach + 1))
    numbers = [
        lookup([order[(order.index(i) + offset) % count] for i in range(count)], index)
        for offset in offsets
    ]
    column_starts = [n * columns for n in numbers]
    row_table = jnp.stack([n * depth for n in numbers])
    column_table = jnp.stack(column_starts)
    odd = jnp.reshape(lax.rem(lax.axis_index("seq"), 2), (1,))
    tokens, odd, row_table, column_table, column_starts = lax.optimization_barrier(
        (tokens, odd, row_table, column_table, column_starts)
    )

    def add(item, chunk, held, sums):
        bring = [i for i in ((1, 2) if item == 0 else (item + 2,)) if i < len(offset_of)]
        bring = [offsets.index(offset_of[i]) for i in bring]
        extra = None
        if item == len(offset_of) - 2:
            bring, extra = [offsets.index(reach)], (w_out, column_table, columns)
        now, held = (held[0], held[1:]) if held else (None, [])
        place = offsets.index(offset_of[item])
        sums, sets, rest = project(
            chunk, row_table, place, weights, now, sums, block, bring, extra
        )
        held = [*held, *sets, *rest]
        return sums, held

    weights = (w_query, w_key, w_value)
    offset_of = [0]
    for step in range(1, reach):
        offset_of += [-step, step]
    windows = 2 * reach - 1
    ahead = {(0, 0): tokens[:half], (0, 1): tokens[half:]}
    behind = dict(ahead)

    def send(slot):
        level, second = divmod(slot - 1, 2)
        up, down = (level, second), (level, 1 - second)
        ahead[level + 1, second] = lax.ppermute(ahead[up], "tp", forward)
        behind[level + 1, 1 - second] = lax.ppermute(behind[down], "tp", backward)

    def halves(offset):
        side = ahead if offset < 0 else behind
        return [side[abs(offset), 0], side[abs(offset), 1]]

    send(1)
    send(2)
    sums, held = add(0, [tokens], [], None)
    for window in range(2, windows):
        level, second = divmod(window, 2)
        up, down = (level, second), (level, 1 - second)
        ahead[up], behind[down], sums, held = lax.optimization_barrier(
            (ahead[up], behind[down], sums, held)
        )
        send(window + 1)
        if window > 2:
            sums, held = add(window - 2, halves(offset_of[window - 2]), held, sums)
    up, down = (reach - 1, 1), (reach - 1, 0)
    ahead[up], behind[down], sums, held = lax.optimization_barrier(
        (ahead[up], behind[down], sums, held)
    )
    for item in (windows - 2, windows - 1):
        sums, held = add(item, halves(offset_of[item]), held, sums)
    final = [*held[0], held[1]]
    ahead, behind = ahead[reach, 0], behind[reach, 1]
    last = [ahead, behind]
    w_query_last, w_key_last, w_value_last, w_first = final
    keys, values, state, sent = finish_keys(
        last, w_key_last, w_value_last, sums[1], sums[2], block, size
    )

    members = lax.axis_size("seq")
    others = [
        lax.ppermute(sent, "seq", [(i, i + shift) for i in range(members - shift)])
        for shift in range(2, members, 2)
    ]
    query, within = finish_query(last, w_query_last, sums[0], keys, values, block, size)
    others, query, within = lax.optimization_barrier((others, query, within))
    share = kernel(
        share_body,
        [(odd, pltpu.SMEM), (state, pltpu.VMEM), *[(other, pltpu.VMEM) for other in others]],
        [(state.shape, BF16)],
    )[0]
    others.append(lax.ppermute(share, "seq", [(i, i ^ 1) for i in range(members)]))

    *parts, top, bottom = attend(query, within, carry, others, w_first, size)

    def partial(rows, offset):
        start = column_starts[offsets.index(offset)]
        return dot(parts[rows], cut_at(w_out, start, columns, 1))

    up = [lax.ppermute(top, "tp", forward), None]
    down = [None, lax.ppermute(bottom, "tp", backward)]
    for distance in range(reach - 1, 0, -1):
        for rows in (0, 1):
            for held, sign, hops in ((up, 1, forward), (down, -1, backward)):
                value = partial(rows, sign * distance)
                if held[rows] is not None:
                    value = value + held[rows].astype(F32)
                held[rows] = lax.ppermute(value.astype(BF16), "tp", hops)
    top_sum = partial(0, 0) + down[0].astype(F32)
    bottom_sum = partial(1, 0) + up[1].astype(F32)
    return finish((top_sum, bottom_sum, up[0], down[1]))


def solution(mesh):
    placed = (
        P("seq", "tp"),
        P(None, "tp"),
        P(None, "tp"),
        P(None, "tp"),
        P("tp", None),
        P("tp", None, None),
    )
    return jax.shard_map(
        local, mesh=mesh, in_specs=placed, out_specs=P("seq", "tp"), check_vma=False
    )
```

```python
import functools

import jax
import jax.numpy as jnp
from jax import lax
from jax.experimental import pallas as pl
from jax.experimental.pallas import tpu as pltpu
from jax.sharding import PartitionSpec as P

EPSILON = 1e-05
BF16 = jnp.bfloat16
F32 = jnp.float32
PROJECT_BYTES = 32 << 20


def ring_order(count):
    columns = 1
    while columns * columns * 4 <= count:
        columns *= 2
    rows = count // columns
    if rows % 2 or columns < 2:
        return list(range(count))
    order = [row * columns for row in range(rows)]
    for step, row in enumerate(reversed(range(rows))):
        span = range(1, columns) if step % 2 == 0 else range(columns - 1, 0, -1)
        order += [row * columns + column for column in span]
    return order


def lookup(table, index):
    value = jnp.int32(table[0])
    for i, entry in enumerate(table[1:], 1):
        value = jnp.where(index == i, jnp.int32(entry), value)
    return value


def cut_at(array, start, size, axis):
    starts = [jnp.int32(0), jnp.int32(0)]
    sizes = list(array.shape)
    starts[axis], sizes[axis] = start, size
    return lax.dynamic_slice(array, starts, sizes, allow_negative_indices=False)


def dot(a, b):
    return jnp.dot(a, b, preferred_element_type=F32)


def dot_rows(a, b):
    return lax.dot_general(a, b, (((0,), (0,)), ((), ())), preferred_element_type=F32)


def dot_columns(a, b):
    return lax.dot_general(a, b, (((1,), (1,)), ((), ())), preferred_element_type=F32)


def kernel(body, inputs, outputs, aliases=None, scratch=(), vmem=16 << 20):
    return pl.pallas_call(
        body,
        in_specs=[pl.BlockSpec(memory_space=space) for _, space in inputs],
        out_specs=[pl.BlockSpec(memory_space=pltpu.VMEM) for _ in outputs],
        out_shape=[jax.ShapeDtypeStruct(shape, kind) for shape, kind in outputs],
        scratch_shapes=list(scratch),
        input_output_aliases=aliases or {},
        compiler_params=pltpu.CompilerParams(vmem_limit_bytes=vmem),
        cost_estimate=pl.CostEstimate(flops=0, bytes_accessed=1 << 20, transcendentals=0),
    )(*[array for array, _ in inputs])


def columns_of(j, block):
    return pl.ds(pl.multiple_of(j * block, block), block)


def project_body(pieces, has_sums, has_rows, block, place, bring, has_columns, *refs):
    starts, xs, refs = refs[0], refs[1 : 1 + pieces], refs[1 + pieces :]
    weights, refs = refs[:3], refs[3:]
    if has_columns:
        (w_out, column_starts), refs = refs[:2], refs[2:]
    held, refs = (refs[:3], refs[3:]) if has_rows else (None, refs)
    sums, refs = (refs[:3], refs[3:]) if has_sums else (None, refs)
    outs, refs = refs[:3], refs[3:]
    wanted, refs = refs[: 3 * len(bring)], refs[3 * len(bring) :]
    depth = xs[0].shape[1]

    def rows_to(k, targets, semaphores, first=0):
        rows = pl.ds(pl.multiple_of(starts[k], depth), depth)
        return [
            pltpu.make_async_copy(weights[i].at[rows, :], targets[i], semaphores.at[first + i])
            for i in range(3)
        ]

    if has_columns:
        target, refs = refs[0], refs[1:]
    brought = []
    for n, k in enumerate(bring):
        brought += rows_to(k, wanted[3 * n : 3 * n + 3], refs[0], 3 * n)
    if has_columns:
        size = target.shape[1]
        cut = pl.ds(pl.multiple_of(column_starts[bring[0]], size), size)
        brought.append(pltpu.make_async_copy(w_out.at[:, cut], target, refs[0].at[3 * len(bring)]))
    copies = []
    if not has_rows:
        held = refs[1:4]
        copies = rows_to(place, held, refs[4])
    for copy in (*copies, *brought):
        copy.start()
    chunk = jnp.concatenate([x[...] for x in xs], 0)
    for copy in copies:
        copy.wait()

    @pl.loop(0, outs[0].shape[1] // block)
    def _(j):
        cut = columns_of(j, block)
        for i in range(3):
            part = dot(chunk, held[i][:, cut])
            outs[i][:, cut] = part if sums is None else sums[i][:, cut] + part

    for copy in brought:
        copy.wait()


def project(chunk, starts, place, weights, held, sums, block, bring, extra=None):
    rows = sum(piece.shape[0] for piece in chunk)
    depth, width = chunk[0].shape[1], weights[0].shape[1]
    inputs = [(starts, pltpu.SMEM)] + [(array, pltpu.VMEM) for array in chunk]
    inputs += [(weight, pltpu.HBM) for weight in weights]
    outputs = [((rows, width), F32)] * 3 + [((depth, width), BF16)] * (3 * len(bring))
    scratch = [pltpu.SemaphoreType.DMA((3 * len(bring) + 1,))]
    if extra is not None:
        w_out, column_starts, columns = extra
        inputs += [(w_out, pltpu.HBM), (column_starts, pltpu.SMEM)]
        outputs += [((w_out.shape[0], columns), BF16)]
    if held is None:
        scratch += [pltpu.VMEM((depth, width), BF16)] * 3 + [pltpu.SemaphoreType.DMA((3,))]
    else:
        inputs += [(weight, pltpu.VMEM) for weight in held]
    aliases = {}
    if sums is not None:
        aliases = {len(inputs) + i: i for i in range(3)}
        inputs += [(s, pltpu.VMEM) for s in sums]
    body = functools.partial(
        project_body,
        len(chunk),
        sums is not None,
        held is not None,
        block,
        place,
        bring,
        extra is not None,
    )
    out = kernel(body, inputs, outputs, aliases, scratch, PROJECT_BYTES)
    sets = [out[3 + 3 * n : 6 + 3 * n] for n in range(len(bring))]
    return out[:3], sets, out[3 + 3 * len(bring) :]


def keys_body(pieces, size, block, *refs):
    xs = refs[:pieces]
    w_key, w_value, key_sum, value_sum, keys_out, values_out, state_out, sent_out = refs[pieces:]
    heads = block // size
    chunk = jnp.concatenate([x[...] for x in xs], 0)
    for j in range(keys_out.shape[1] // block):
        cut = slice(j * block, (j + 1) * block)
        keys = (key_sum[:, cut] + dot(chunk, w_key[:, cut])).astype(BF16)
        keys_out[:, cut] = keys
        values = (value_sum[:, cut] + dot(chunk, w_value[:, cut])).astype(BF16)
        values_out[:, cut] = values
        states = dot_rows(keys, values)
        for h in range(heads):
            own = slice(h * size, (h + 1) * size)
            state_out[j * heads + h] = states[own, own]
            sent_out[j * heads + h] = states[own, own].astype(BF16)


def finish_keys(chunk, w_key, w_value, key_sum, value_sum, block, size):
    rows, width = key_sum.shape
    arrays = (*chunk, w_key, w_value, key_sum, value_sum)
    outputs = [((rows, width), BF16)] * 2
    outputs += [((width // size, size, size), kind) for kind in (F32, BF16)]
    body = functools.partial(keys_body, len(chunk), size, block)
    return kernel(body, [(array, pltpu.VMEM) for array in arrays], outputs)


def within_body(pieces, size, block, *refs):
    xs = refs[:pieces]
    w_query, query_sum, keys_in, values_in, query_out, within_out = refs[pieces:]
    rows, width = query_sum.shape
    chunk = jnp.concatenate([x[...] for x in xs], 0)
    tile = rows // 2
    causal = lax.broadcasted_iota(jnp.int32, (tile, tile), 0) >= lax.broadcasted_iota(
        jnp.int32, (tile, tile), 1
    )

    for j in range(width // block):
        cut = slice(j * block, (j + 1) * block)
        query = (query_sum[:, cut] + dot(chunk, w_query[:, cut])).astype(BF16)
        query_out[:, cut] = query
        keys, values = keys_in[:, cut], values_in[:, cut]
        sums = []
        for h in range(block // size):
            own = slice(h * size, (h + 1) * size)
            q, k, v = query[:, own], keys[:, own], values[:, own]
            first = jnp.where(causal, dot_columns(q[:tile], k[:tile]), 0.0).astype(BF16)
            lower = dot_columns(q[tile:], k[:tile]).astype(BF16)
            second = jnp.where(causal, dot_columns(q[tile:], k[tile:]), 0.0).astype(BF16)
            bottom = dot(lower, v[:tile]) + dot(second, v[tile:])
            sums.append(jnp.concatenate([dot(first, v[:tile]), bottom], 0))
        within_out[:, cut] = jnp.concatenate(sums, 1)


def finish_query(chunk, w_query, query_sum, keys, values, block, size):
    arrays = (*chunk, w_query, query_sum, keys, values)
    outputs = [(query_sum.shape, BF16), (query_sum.shape, F32)]
    body = functools.partial(within_body, len(chunk), size, block)
    return kernel(body, [(array, pltpu.VMEM) for array in arrays], outputs)


def attend_body(earlier, size, query, within, carry, *refs):
    others = refs[:earlier]
    w_first, top_out, bottom_out, top_first, bottom_first = refs[earlier:]
    heads = carry.shape[0]
    half = query.shape[0] // 2
    for h in range(heads):
        cut = slice(h * size, (h + 1) * size)
        prior = carry[h]
        for other in others:
            prior = prior + other[h].astype(F32)
        high = prior.astype(BF16)
        low = (prior - high.astype(F32)).astype(BF16)
        q = query[:, cut]
        o = within[:, cut] + dot(jnp.concatenate([q, q], 1), jnp.concatenate([high, low], 0))
        o = o * lax.rsqrt(jnp.mean(o * o, axis=-1, keepdims=True) + EPSILON)
        attended = o.astype(BF16)
        top_out[:, cut] = attended[:half]
        bottom_out[:, cut] = attended[half:]
    block = 256 if w_first.shape[1] % 256 == 0 else 128

    for j in range(w_first.shape[1] // block):
        cut = slice(j * block, (j + 1) * block)
        weight = w_first[:, cut]
        top_first[:, cut] = dot(top_out[...], weight).astype(BF16)
        bottom_first[:, cut] = dot(bottom_out[...], weight).astype(BF16)


def attend(query, within, carry, others, w_first, size):
    rows, width = query.shape
    inputs = [(s, pltpu.VMEM) for s in (query, within, carry, *others, w_first)]
    outputs = [((rows // 2, width), BF16)] * 2 + [((rows // 2, w_first.shape[1]), BF16)] * 2
    return kernel(functools.partial(attend_body, len(others), size), inputs, outputs)


def share_body(odd, own, *refs):
    *others, out = refs
    total = jnp.where(odd[0] == 1, 0.0, own[...])
    for other in others:
        total = total + other[...].astype(F32)
    out[...] = total.astype(BF16)


def finish_body(top_sum, bottom_sum, top, bottom, out, staged, moved):
    half, parts = top.shape[0], moved.shape[1]
    rows = half // parts
    copies = []
    for i, (total, last) in enumerate(((top_sum, top), (bottom_sum, bottom))):
        for p in range(parts):
            mine = slice(p * rows, (p + 1) * rows)
            cut = slice(i * half + p * rows, i * half + (p + 1) * rows)
            staged[cut] = (total[mine] + last[mine].astype(F32)).astype(BF16)
            copies.append(pltpu.make_async_copy(staged.at[cut, :], out.at[cut, :], moved.at[i, p]))
            copies[-1].start()
    for copy in copies:
        copy.wait()


def finish(arrays):
    shape = (2 * arrays[0].shape[0], arrays[0].shape[1])
    return pl.pallas_call(
        finish_body,
        in_specs=[pl.BlockSpec(memory_space=pltpu.VMEM)] * 4,
        out_specs=pl.BlockSpec(memory_space=pltpu.HBM),
        out_shape=jax.ShapeDtypeStruct(shape, BF16),
        scratch_shapes=[pltpu.VMEM(shape, BF16), pltpu.SemaphoreType.DMA((2, 4))],
        compiler_params=pltpu.CompilerParams(vmem_limit_bytes=16 << 20),
        cost_estimate=pl.CostEstimate(flops=0, bytes_accessed=1 << 20, transcendentals=0),
    )(*arrays)


def local(tokens, w_query, w_key, w_value, w_out, carry):
    row_count = tokens.shape[0]
    head_count, size = carry.shape[:2]
    block = size * (2 if head_count % 2 == 0 else 1)
    half = row_count // 2
    count = lax.axis_size("tp")
    reach = count // 2
    order = ring_order(count)
    forward = [(order[i], order[(i + 1) % count]) for i in range(count)]
    backward = [(b, a) for a, b in forward]
    index = lax.axis_index("tp")
    depth = tokens.shape[1]
    columns = w_out.shape[1] // count

    offsets = list(range(-reach + 1, reach + 1))
    numbers = [
        lookup([order[(order.index(i) + offset) % count] for i in range(count)], index)
        for offset in offsets
    ]
    column_starts = [n * columns for n in numbers]
    row_table = jnp.stack([n * depth for n in numbers])
    column_table = jnp.stack(column_starts)
    odd = jnp.reshape(lax.rem(lax.axis_index("seq"), 2), (1,))
    tokens, odd, row_table, column_table, column_starts = lax.optimization_barrier(
        (tokens, odd, row_table, column_table, column_starts)
    )

    def add(item, chunk, held, sums):
        bring = [i for i in ((1, 2) if item == 0 else (item + 2,)) if i < len(offset_of)]
        bring = [offsets.index(offset_of[i]) for i in bring]
        extra = None
        if item == len(offset_of) - 2:
            bring, extra = [offsets.index(reach)], (w_out, column_table, columns)
        now, held = (held[0], held[1:]) if held else (None, [])
        place = offsets.index(offset_of[item])
        sums, sets, rest = project(
            chunk, row_table, place, weights, now, sums, block, bring, extra
        )
        held = [*held, *sets, *rest]
        return sums, held

    weights = (w_query, w_key, w_value)
    offset_of = [0]
    for step in range(1, reach):
        offset_of += [-step, step]
    windows = 2 * reach - 1
    ahead = {(0, 0): tokens[:half], (0, 1): tokens[half:]}
    behind = dict(ahead)

    def send(slot):
        level, second = divmod(slot - 1, 2)
        up, down = (level, second), (level, 1 - second)
        ahead[level + 1, second] = lax.ppermute(ahead[up], "tp", forward)
        behind[level + 1, 1 - second] = lax.ppermute(behind[down], "tp", backward)

    def halves(offset):
        side = ahead if offset < 0 else behind
        return [side[abs(offset), 0], side[abs(offset), 1]]

    send(1)
    send(2)
    sums, held = add(0, halves(0), [], None)
    for window in range(2, windows):
        level, second = divmod(window, 2)
        up, down = (level, second), (level, 1 - second)
        ahead[up], behind[down], sums, held = lax.optimization_barrier(
            (ahead[up], behind[down], sums, held)
        )
        send(window + 1)
        if window > 2:
            sums, held = add(window - 2, halves(offset_of[window - 2]), held, sums)
    up, down = (reach - 1, 1), (reach - 1, 0)
    ahead[up], behind[down], sums, held = lax.optimization_barrier(
        (ahead[up], behind[down], sums, held)
    )
    for item in (windows - 2, windows - 1):
        sums, held = add(item, halves(offset_of[item]), held, sums)
    final = [*held[0], held[1]]
    ahead, behind = ahead[reach, 0], behind[reach, 1]
    last = [ahead, behind]
    w_query_last, w_key_last, w_value_last, w_first = final
    keys, values, state, sent = finish_keys(
        last, w_key_last, w_value_last, sums[1], sums[2], block, size
    )

    members = lax.axis_size("seq")
    others = [
        lax.ppermute(sent, "seq", [(i, i + shift) for i in range(members - shift)])
        for shift in range(2, members, 2)
    ]
    query, within = finish_query(last, w_query_last, sums[0], keys, values, block, size)
    others, query, within = lax.optimization_barrier((others, query, within))
    share = kernel(
        share_body,
        [(odd, pltpu.SMEM), (state, pltpu.VMEM), *[(other, pltpu.VMEM) for other in others]],
        [(state.shape, BF16)],
    )[0]
    others.append(lax.ppermute(share, "seq", [(i, i ^ 1) for i in range(members)]))

    *parts, top, bottom = attend(query, within, carry, others, w_first, size)

    def partial(rows, offset):
        start = column_starts[offsets.index(offset)]
        return dot(parts[rows], cut_at(w_out, start, columns, 1))

    up = [lax.ppermute(top, "tp", forward), None]
    down = [None, lax.ppermute(bottom, "tp", backward)]
    for distance in range(reach - 1, 0, -1):
        for rows in (0, 1):
            for held, sign, hops in ((up, 1, forward), (down, -1, backward)):
                value = partial(rows, sign * distance)
                if held[rows] is not None:
                    value = value + held[rows].astype(F32)
                held[rows] = lax.ppermute(value.astype(BF16), "tp", hops)
    top_sum = partial(0, 0) + down[0].astype(F32)
    bottom_sum = partial(1, 0) + up[1].astype(F32)
    return finish((top_sum, bottom_sum, up[0], down[1]))


def solution(mesh):
    placed = (
        P("seq", "tp"),
        P(None, "tp"),
        P(None, "tp"),
        P(None, "tp"),
        P("tp", None),
        P("tp", None, None),
    )
    return jax.shard_map(
        local, mesh=mesh, in_specs=placed, out_specs=P("seq", "tp"), check_vma=False
    )
```

```python
import functools

import jax
import jax.numpy as jnp
from jax import lax
from jax.experimental import pallas as pl
from jax.experimental.pallas import tpu as pltpu
from jax.sharding import PartitionSpec as P

EPSILON = 1e-05
BF16 = jnp.bfloat16
F32 = jnp.float32
PROJECT_BYTES = 32 << 20


def ring_order(count):
    columns = 1
    while columns * columns * 4 <= count:
        columns *= 2
    rows = count // columns
    if rows % 2 or columns < 2:
        return list(range(count))
    order = [row * columns for row in range(rows)]
    for step, row in enumerate(reversed(range(rows))):
        span = range(1, columns) if step % 2 == 0 else range(columns - 1, 0, -1)
        order += [row * columns + column for column in span]
    return order


def lookup(table, index):
    value = jnp.int32(table[0])
    for i, entry in enumerate(table[1:], 1):
        value = jnp.where(index == i, jnp.int32(entry), value)
    return value


def cut_at(array, start, size, axis):
    starts = [jnp.int32(0), jnp.int32(0)]
    sizes = list(array.shape)
    starts[axis], sizes[axis] = start, size
    return lax.dynamic_slice(array, starts, sizes, allow_negative_indices=False)


def dot(a, b):
    return jnp.dot(a, b, preferred_element_type=F32)


def dot_rows(a, b):
    return lax.dot_general(a, b, (((0,), (0,)), ((), ())), preferred_element_type=F32)


def dot_columns(a, b):
    return lax.dot_general(a, b, (((1,), (1,)), ((), ())), preferred_element_type=F32)


def kernel(body, inputs, outputs, aliases=None, scratch=(), vmem=16 << 20):
    return pl.pallas_call(
        body,
        in_specs=[pl.BlockSpec(memory_space=space) for _, space in inputs],
        out_specs=[pl.BlockSpec(memory_space=pltpu.VMEM) for _ in outputs],
        out_shape=[jax.ShapeDtypeStruct(shape, kind) for shape, kind in outputs],
        scratch_shapes=list(scratch),
        input_output_aliases=aliases or {},
        compiler_params=pltpu.CompilerParams(vmem_limit_bytes=vmem),
        cost_estimate=pl.CostEstimate(flops=0, bytes_accessed=1 << 20, transcendentals=0),
    )(*[array for array, _ in inputs])


def columns_of(j, block):
    return pl.ds(pl.multiple_of(j * block, block), block)


def project_body(pieces, has_sums, has_rows, block, place, bring, has_columns, *refs):
    starts, xs, refs = refs[0], refs[1 : 1 + pieces], refs[1 + pieces :]
    weights, refs = refs[:3], refs[3:]
    if has_columns:
        (w_out, column_starts), refs = refs[:2], refs[2:]
    held, refs = (refs[:3], refs[3:]) if has_rows else (None, refs)
    sums, refs = (refs[:3], refs[3:]) if has_sums else (None, refs)
    outs, refs = refs[:3], refs[3:]
    wanted, refs = refs[: 3 * len(bring)], refs[3 * len(bring) :]
    depth = xs[0].shape[1]

    def rows_to(k, targets, semaphores, first=0):
        rows = pl.ds(pl.multiple_of(starts[k], depth), depth)
        return [
            pltpu.make_async_copy(weights[i].at[rows, :], targets[i], semaphores.at[first + i])
            for i in range(3)
        ]

    if has_columns:
        target, refs = refs[0], refs[1:]
    brought = []
    for n, k in enumerate(bring):
        brought += rows_to(k, wanted[3 * n : 3 * n + 3], refs[0], 3 * n)
    if has_columns:
        size = target.shape[1]
        cut = pl.ds(pl.multiple_of(column_starts[bring[0]], size), size)
        brought.append(pltpu.make_async_copy(w_out.at[:, cut], target, refs[0].at[3 * len(bring)]))
    copies = []
    if not has_rows:
        held = refs[1:4]
        copies = rows_to(place, held, refs[4])
    for copy in (*copies, *brought):
        copy.start()
    chunk = jnp.concatenate([x[...] for x in xs], 0)
    for copy in copies:
        copy.wait()

    @pl.loop(0, outs[0].shape[1] // block)
    def _(j):
        cut = columns_of(j, block)
        for i in range(3):
            part = dot(chunk, held[i][:, cut])
            outs[i][:, cut] = part if sums is None else sums[i][:, cut] + part

    for copy in brought:
        copy.wait()


def project(chunk, starts, place, weights, held, sums, block, bring, extra=None):
    rows = sum(piece.shape[0] for piece in chunk)
    depth, width = chunk[0].shape[1], weights[0].shape[1]
    inputs = [(starts, pltpu.SMEM)] + [(array, pltpu.VMEM) for array in chunk]
    inputs += [(weight, pltpu.HBM) for weight in weights]
    outputs = [((rows, width), F32)] * 3 + [((depth, width), BF16)] * (3 * len(bring))
    scratch = [pltpu.SemaphoreType.DMA((3 * len(bring) + 1,))]
    if extra is not None:
        w_out, column_starts, columns = extra
        inputs += [(w_out, pltpu.HBM), (column_starts, pltpu.SMEM)]
        outputs += [((w_out.shape[0], columns), BF16)]
    if held is None:
        scratch += [pltpu.VMEM((depth, width), BF16)] * 3 + [pltpu.SemaphoreType.DMA((3,))]
    else:
        inputs += [(weight, pltpu.VMEM) for weight in held]
    aliases = {}
    if sums is not None:
        aliases = {len(inputs) + i: i for i in range(3)}
        inputs += [(s, pltpu.VMEM) for s in sums]
    body = functools.partial(
        project_body,
        len(chunk),
        sums is not None,
        held is not None,
        block,
        place,
        bring,
        extra is not None,
    )
    out = kernel(body, inputs, outputs, aliases, scratch, PROJECT_BYTES)
    sets = [out[3 + 3 * n : 6 + 3 * n] for n in range(len(bring))]
    return out[:3], sets, out[3 + 3 * len(bring) :]


def keys_body(pieces, size, block, *refs):
    xs = refs[:pieces]
    w_key, w_value, key_sum, value_sum, keys_out, values_out, state_out, sent_out = refs[pieces:]
    heads = block // size
    chunk = jnp.concatenate([x[...] for x in xs], 0)
    for j in range(keys_out.shape[1] // block):
        cut = slice(j * block, (j + 1) * block)
        keys = (key_sum[:, cut] + dot(chunk, w_key[:, cut])).astype(BF16)
        keys_out[:, cut] = keys
        values = (value_sum[:, cut] + dot(chunk, w_value[:, cut])).astype(BF16)
        values_out[:, cut] = values
        states = dot_rows(keys, values)
        for h in range(heads):
            own = slice(h * size, (h + 1) * size)
            state_out[j * heads + h] = states[own, own]
            sent_out[j * heads + h] = states[own, own].astype(BF16)


def finish_keys(chunk, w_key, w_value, key_sum, value_sum, block, size):
    rows, width = key_sum.shape
    arrays = (*chunk, w_key, w_value, key_sum, value_sum)
    outputs = [((rows, width), BF16)] * 2
    outputs += [((width // size, size, size), kind) for kind in (F32, BF16)]
    body = functools.partial(keys_body, len(chunk), size, block)
    return kernel(body, [(array, pltpu.VMEM) for array in arrays], outputs)


def within_body(pieces, size, block, *refs):
    xs = refs[:pieces]
    w_query, query_sum, keys_in, values_in, query_out, within_out = refs[pieces:]
    rows, width = query_sum.shape
    chunk = jnp.concatenate([x[...] for x in xs], 0)
    tile = rows // 2
    causal = lax.broadcasted_iota(jnp.int32, (tile, tile), 0) >= lax.broadcasted_iota(
        jnp.int32, (tile, tile), 1
    )

    for j in range(width // block):
        cut = slice(j * block, (j + 1) * block)
        query = (query_sum[:, cut] + dot(chunk, w_query[:, cut])).astype(BF16)
        query_out[:, cut] = query
        keys, values = keys_in[:, cut], values_in[:, cut]
        sums = []
        for h in range(block // size):
            own = slice(h * size, (h + 1) * size)
            q, k, v = query[:, own], keys[:, own], values[:, own]
            first = jnp.where(causal, dot_columns(q[:tile], k[:tile]), 0.0).astype(BF16)
            lower = dot_columns(q[tile:], k[:tile]).astype(BF16)
            second = jnp.where(causal, dot_columns(q[tile:], k[tile:]), 0.0).astype(BF16)
            bottom = dot(lower, v[:tile]) + dot(second, v[tile:])
            sums.append(jnp.concatenate([dot(first, v[:tile]), bottom], 0))
        within_out[:, cut] = jnp.concatenate(sums, 1)


def finish_query(chunk, w_query, query_sum, keys, values, block, size):
    arrays = (*chunk, w_query, query_sum, keys, values)
    outputs = [(query_sum.shape, BF16), (query_sum.shape, F32)]
    body = functools.partial(within_body, len(chunk), size, block)
    return kernel(body, [(array, pltpu.VMEM) for array in arrays], outputs)


def attend_body(earlier, size, query, within, carry, *refs):
    others = refs[:earlier]
    w_first, top_out, bottom_out, top_first, bottom_first = refs[earlier:]
    heads = carry.shape[0]
    half = query.shape[0] // 2
    for h in range(heads):
        cut = slice(h * size, (h + 1) * size)
        prior = carry[h]
        for other in others:
            prior = prior + other[h].astype(F32)
        high = prior.astype(BF16)
        low = (prior - high.astype(F32)).astype(BF16)
        q = query[:, cut]
        o = within[:, cut] + dot(jnp.concatenate([q, q], 1), jnp.concatenate([high, low], 0))
        o = o * lax.rsqrt(jnp.mean(o * o, axis=-1, keepdims=True) + EPSILON)
        attended = o.astype(BF16)
        top_out[:, cut] = attended[:half]
        bottom_out[:, cut] = attended[half:]
    block = 256 if w_first.shape[1] % 256 == 0 else 128

    for j in range(w_first.shape[1] // block):
        cut = slice(j * block, (j + 1) * block)
        weight = w_first[:, cut]
        top_first[:, cut] = dot(top_out[...], weight).astype(BF16)
        bottom_first[:, cut] = dot(bottom_out[...], weight).astype(BF16)


def attend(query, within, carry, others, w_first, size):
    rows, width = query.shape
    inputs = [(s, pltpu.VMEM) for s in (query, within, carry, *others, w_first)]
    outputs = [((rows // 2, width), BF16)] * 2 + [((rows // 2, w_first.shape[1]), BF16)] * 2
    return kernel(functools.partial(attend_body, len(others), size), inputs, outputs)


def share_body(odd, own, *refs):
    *others, out = refs
    total = jnp.where(odd[0] == 1, 0.0, own[...])
    for other in others:
        total = total + other[...].astype(F32)
    out[...] = total.astype(BF16)


def finish_body(top_sum, bottom_sum, top, bottom, out, staged, moved):
    half, parts = top.shape[0], moved.shape[1]
    rows = half // parts
    copies = []
    for i, (total, last) in enumerate(((top_sum, top), (bottom_sum, bottom))):
        for p in range(parts):
            mine = slice(p * rows, (p + 1) * rows)
            cut = slice(i * half + p * rows, i * half + (p + 1) * rows)
            staged[cut] = (total[mine] + last[mine].astype(F32)).astype(BF16)
            copies.append(pltpu.make_async_copy(staged.at[cut, :], out.at[cut, :], moved.at[i, p]))
            copies[-1].start()
    for copy in copies:
        copy.wait()


def finish(arrays):
    shape = (2 * arrays[0].shape[0], arrays[0].shape[1])
    return pl.pallas_call(
        finish_body,
        in_specs=[pl.BlockSpec(memory_space=pltpu.VMEM)] * 4,
        out_specs=pl.BlockSpec(memory_space=pltpu.HBM),
        out_shape=jax.ShapeDtypeStruct(shape, BF16),
        scratch_shapes=[pltpu.VMEM(shape, BF16), pltpu.SemaphoreType.DMA((2, 4))],
        compiler_params=pltpu.CompilerParams(vmem_limit_bytes=16 << 20),
        cost_estimate=pl.CostEstimate(flops=0, bytes_accessed=1 << 20, transcendentals=0),
    )(*arrays)


def local(tokens, w_query, w_key, w_value, w_out, carry):
    row_count = tokens.shape[0]
    head_count, size = carry.shape[:2]
    block = size * (2 if head_count % 2 == 0 else 1)
    half = row_count // 2
    count = lax.axis_size("tp")
    reach = count // 2
    order = ring_order(count)[::-1]
    forward = [(order[i], order[(i + 1) % count]) for i in range(count)]
    backward = [(b, a) for a, b in forward]
    index = lax.axis_index("tp")
    depth = tokens.shape[1]
    columns = w_out.shape[1] // count

    offsets = list(range(-reach + 1, reach + 1))
    numbers = [
        lookup([order[(order.index(i) + offset) % count] for i in range(count)], index)
        for offset in offsets
    ]
    column_starts = [n * columns for n in numbers]
    row_table = jnp.stack([n * depth for n in numbers])
    column_table = jnp.stack(column_starts)
    odd = jnp.reshape(lax.rem(lax.axis_index("seq"), 2), (1,))
    tokens, odd, row_table, column_table, column_starts = lax.optimization_barrier(
        (tokens, odd, row_table, column_table, column_starts)
    )

    def add(item, chunk, held, sums):
        bring = [i for i in ((1, 2) if item == 0 else (item + 2,)) if i < len(offset_of)]
        bring = [offsets.index(offset_of[i]) for i in bring]
        extra = None
        if item == len(offset_of) - 2:
            bring, extra = [offsets.index(reach)], (w_out, column_table, columns)
        now, held = (held[0], held[1:]) if held else (None, [])
        place = offsets.index(offset_of[item])
        sums, sets, rest = project(
            chunk, row_table, place, weights, now, sums, block, bring, extra
        )
        held = [*held, *sets, *rest]
        return sums, held

    weights = (w_query, w_key, w_value)
    offset_of = [0]
    for step in range(1, reach):
        offset_of += [-step, step]
    windows = 2 * reach - 1
    ahead = {(0, 0): tokens[:half], (0, 1): tokens[half:]}
    behind = dict(ahead)

    def send(slot):
        level, second = divmod(slot - 1, 2)
        up, down = (level, second), (level, 1 - second)
        ahead[level + 1, second] = lax.ppermute(ahead[up], "tp", forward)
        behind[level + 1, 1 - second] = lax.ppermute(behind[down], "tp", backward)

    def halves(offset):
        side = ahead if offset < 0 else behind
        return [side[abs(offset), 0], side[abs(offset), 1]]

    send(1)
    send(2)
    sums, held = add(0, halves(0), [], None)
    for window in range(2, windows):
        level, second = divmod(window, 2)
        up, down = (level, second), (level, 1 - second)
        ahead[up], behind[down], sums, held = lax.optimization_barrier(
            (ahead[up], behind[down], sums, held)
        )
        send(window + 1)
        if window > 2:
            sums, held = add(window - 2, halves(offset_of[window - 2]), held, sums)
    up, down = (reach - 1, 1), (reach - 1, 0)
    ahead[up], behind[down], sums, held = lax.optimization_barrier(
        (ahead[up], behind[down], sums, held)
    )
    for item in (windows - 2, windows - 1):
        sums, held = add(item, halves(offset_of[item]), held, sums)
    final = [*held[0], held[1]]
    ahead, behind = ahead[reach, 0], behind[reach, 1]
    last = [ahead, behind]
    w_query_last, w_key_last, w_value_last, w_first = final
    keys, values, state, sent = finish_keys(
        last, w_key_last, w_value_last, sums[1], sums[2], block, size
    )

    members = lax.axis_size("seq")
    others = [
        lax.ppermute(sent, "seq", [(i, i + shift) for i in range(members - shift)])
        for shift in range(2, members, 2)
    ]
    query, within = finish_query(last, w_query_last, sums[0], keys, values, block, size)
    others, query, within = lax.optimization_barrier((others, query, within))
    share = kernel(
        share_body,
        [(odd, pltpu.SMEM), (state, pltpu.VMEM), *[(other, pltpu.VMEM) for other in others]],
        [(state.shape, BF16)],
    )[0]
    others.append(lax.ppermute(share, "seq", [(i, i ^ 1) for i in range(members)]))

    *parts, top, bottom = attend(query, within, carry, others, w_first, size)

    def partial(rows, offset):
        start = column_starts[offsets.index(offset)]
        return dot(parts[rows], cut_at(w_out, start, columns, 1))

    up = [lax.ppermute(top, "tp", forward), None]
    down = [None, lax.ppermute(bottom, "tp", backward)]
    for distance in range(reach - 1, 0, -1):
        for rows in (0, 1):
            for held, sign, hops in ((up, 1, forward), (down, -1, backward)):
                value = partial(rows, sign * distance)
                if held[rows] is not None:
                    value = value + held[rows].astype(F32)
                held[rows] = lax.ppermute(value.astype(BF16), "tp", hops)
    top_sum = partial(0, 0) + down[0].astype(F32)
    bottom_sum = partial(1, 0) + up[1].astype(F32)
    return finish((top_sum, bottom_sum, up[0], down[1]))


def solution(mesh):
    placed = (
        P("seq", "tp"),
        P(None, "tp"),
        P(None, "tp"),
        P(None, "tp"),
        P("tp", None),
        P("tp", None, None),
    )
    return jax.shard_map(
        local, mesh=mesh, in_specs=placed, out_specs=P("seq", "tp"), check_vma=False
    )
```

```python
import functools

import jax
import jax.numpy as jnp
from jax import lax
from jax.experimental import pallas as pl
from jax.experimental.pallas import tpu as pltpu
from jax.sharding import PartitionSpec as P

EPSILON = 1e-05
BF16 = jnp.bfloat16
F32 = jnp.float32
PROJECT_BYTES = 32 << 20


def ring_order(count):
    columns = 1
    while columns * columns * 4 <= count:
        columns *= 2
    rows = count // columns
    if rows % 2 or columns < 2:
        return list(range(count))
    order = [row * columns for row in range(rows)]
    for step, row in enumerate(reversed(range(rows))):
        span = range(1, columns) if step % 2 == 0 else range(columns - 1, 0, -1)
        order += [row * columns + column for column in span]
    return order


def lookup(table, index):
    value = jnp.int32(table[0])
    for i, entry in enumerate(table[1:], 1):
        value = jnp.where(index == i, jnp.int32(entry), value)
    return value


def cut_at(array, start, size, axis):
    starts = [jnp.int32(0), jnp.int32(0)]
    sizes = list(array.shape)
    starts[axis], sizes[axis] = start, size
    return lax.dynamic_slice(array, starts, sizes, allow_negative_indices=False)


def dot(a, b):
    return jnp.dot(a, b, preferred_element_type=F32)


def dot_rows(a, b):
    return lax.dot_general(a, b, (((0,), (0,)), ((), ())), preferred_element_type=F32)


def dot_columns(a, b):
    return lax.dot_general(a, b, (((1,), (1,)), ((), ())), preferred_element_type=F32)


def kernel(body, inputs, outputs, aliases=None, scratch=(), vmem=16 << 20):
    return pl.pallas_call(
        body,
        in_specs=[pl.BlockSpec(memory_space=space) for _, space in inputs],
        out_specs=[pl.BlockSpec(memory_space=pltpu.VMEM) for _ in outputs],
        out_shape=[jax.ShapeDtypeStruct(shape, kind) for shape, kind in outputs],
        scratch_shapes=list(scratch),
        input_output_aliases=aliases or {},
        compiler_params=pltpu.CompilerParams(vmem_limit_bytes=vmem),
        cost_estimate=pl.CostEstimate(flops=0, bytes_accessed=1 << 20, transcendentals=0),
    )(*[array for array, _ in inputs])


def columns_of(j, block):
    return pl.ds(pl.multiple_of(j * block, block), block)


def project_body(pieces, has_sums, has_rows, block, place, bring, has_columns, *refs):
    starts, xs, refs = refs[0], refs[1 : 1 + pieces], refs[1 + pieces :]
    weights, refs = refs[:3], refs[3:]
    if has_columns:
        (w_out, column_starts), refs = refs[:2], refs[2:]
    held, refs = (refs[:3], refs[3:]) if has_rows else (None, refs)
    sums, refs = (refs[:3], refs[3:]) if has_sums else (None, refs)
    outs, refs = refs[:3], refs[3:]
    wanted, refs = refs[: 3 * len(bring)], refs[3 * len(bring) :]
    depth = xs[0].shape[1]

    def rows_to(k, targets, semaphores, first=0):
        rows = pl.ds(pl.multiple_of(starts[k], depth), depth)
        return [
            pltpu.make_async_copy(weights[i].at[rows, :], targets[i], semaphores.at[first + i])
            for i in range(3)
        ]

    if has_columns:
        target, refs = refs[0], refs[1:]
    brought = []
    for n, k in enumerate(bring):
        brought += rows_to(k, wanted[3 * n : 3 * n + 3], refs[0], 3 * n)
    if has_columns:
        size = target.shape[1]
        cut = pl.ds(pl.multiple_of(column_starts[bring[0]], size), size)
        brought.append(pltpu.make_async_copy(w_out.at[:, cut], target, refs[0].at[3 * len(bring)]))
    copies = []
    if not has_rows:
        held = refs[1:4]
        copies = rows_to(place, held, refs[4])
    for copy in (*copies, *brought):
        copy.start()
    chunk = jnp.concatenate([x[...] for x in xs], 0)
    for copy in copies:
        copy.wait()

    @pl.loop(0, outs[0].shape[1] // block)
    def _(j):
        cut = columns_of(j, block)
        for i in range(3):
            part = dot(chunk, held[i][:, cut])
            outs[i][:, cut] = part if sums is None else sums[i][:, cut] + part

    for copy in brought:
        copy.wait()


def project(chunk, starts, place, weights, held, sums, block, bring, extra=None):
    rows = sum(piece.shape[0] for piece in chunk)
    depth, width = chunk[0].shape[1], weights[0].shape[1]
    inputs = [(starts, pltpu.SMEM)] + [(array, pltpu.VMEM) for array in chunk]
    inputs += [(weight, pltpu.HBM) for weight in weights]
    outputs = [((rows, width), F32)] * 3 + [((depth, width), BF16)] * (3 * len(bring))
    scratch = [pltpu.SemaphoreType.DMA((3 * len(bring) + 1,))]
    if extra is not None:
        w_out, column_starts, columns = extra
        inputs += [(w_out, pltpu.HBM), (column_starts, pltpu.SMEM)]
        outputs += [((w_out.shape[0], columns), BF16)]
    if held is None:
        scratch += [pltpu.VMEM((depth, width), BF16)] * 3 + [pltpu.SemaphoreType.DMA((3,))]
    else:
        inputs += [(weight, pltpu.VMEM) for weight in held]
    aliases = {}
    if sums is not None:
        aliases = {len(inputs) + i: i for i in range(3)}
        inputs += [(s, pltpu.VMEM) for s in sums]
    body = functools.partial(
        project_body,
        len(chunk),
        sums is not None,
        held is not None,
        block,
        place,
        bring,
        extra is not None,
    )
    out = kernel(body, inputs, outputs, aliases, scratch, PROJECT_BYTES)
    sets = [out[3 + 3 * n : 6 + 3 * n] for n in range(len(bring))]
    return out[:3], sets, out[3 + 3 * len(bring) :]


def keys_body(part, size, block, has_state, x, *refs):
    w_key, w_value, key_sum, value_sum, *refs = refs
    if has_state:
        state_in, *refs = refs
        keys_out, values_out, state_out, sent_out = refs
    else:
        keys_out, values_out, state_out = refs
    rows = x.shape[0]
    mine = slice(part * rows, (part + 1) * rows)
    heads = block // size
    for j in range(keys_out.shape[1] // block):
        cut = slice(j * block, (j + 1) * block)
        keys = (key_sum[mine, cut] + dot(x[...], w_key[:, cut])).astype(BF16)
        keys_out[:, cut] = keys
        values = (value_sum[mine, cut] + dot(x[...], w_value[:, cut])).astype(BF16)
        values_out[:, cut] = values
        states = dot_rows(keys, values)
        for h in range(heads):
            own = slice(h * size, (h + 1) * size)
            state = states[own, own]
            if has_state:
                state = state + state_in[j * heads + h]
                sent_out[j * heads + h] = state.astype(BF16)
            state_out[j * heads + h] = state


def finish_keys(x, part, w_key, w_value, key_sum, value_sum, state, block, size):
    rows, width = x.shape[0], w_key.shape[1]
    arrays = [x, w_key, w_value, key_sum, value_sum] + ([] if state is None else [state])
    shape = (width // size, size, size)
    outputs = [((rows, width), BF16)] * 2 + [(shape, F32)]
    outputs += [] if state is None else [(shape, BF16)]
    body = functools.partial(keys_body, part, size, block, state is not None)
    return kernel(body, [(array, pltpu.VMEM) for array in arrays], outputs)


def within_body(pieces, size, block, *refs):
    xs = refs[:pieces]
    w_query, query_sum, *halves, query_out, within_out = refs[pieces:]
    rows, width = query_sum.shape
    chunk = jnp.concatenate([x[...] for x in xs], 0)
    tile = rows // 2
    causal = lax.broadcasted_iota(jnp.int32, (tile, tile), 0) >= lax.broadcasted_iota(
        jnp.int32, (tile, tile), 1
    )

    for j in range(width // block):
        cut = slice(j * block, (j + 1) * block)
        query = (query_sum[:, cut] + dot(chunk, w_query[:, cut])).astype(BF16)
        query_out[:, cut] = query
        (k_top, k_bottom), (v_top, v_bottom) = [
            [half[:, cut] for half in pair] for pair in (halves[:2], halves[2:])
        ]
        sums = []
        for h in range(block // size):
            own = slice(h * size, (h + 1) * size)
            q = query[:, own]
            first = jnp.where(causal, dot_columns(q[:tile], k_top[:, own]), 0.0).astype(BF16)
            lower = dot_columns(q[tile:], k_top[:, own]).astype(BF16)
            second = jnp.where(causal, dot_columns(q[tile:], k_bottom[:, own]), 0.0).astype(BF16)
            bottom = dot(lower, v_top[:, own]) + dot(second, v_bottom[:, own])
            sums.append(jnp.concatenate([dot(first, v_top[:, own]), bottom], 0))
        within_out[:, cut] = jnp.concatenate(sums, 1)


def finish_query(chunk, w_query, query_sum, keys, values, block, size):
    arrays = (*chunk, w_query, query_sum, *keys, *values)
    outputs = [(query_sum.shape, BF16), (query_sum.shape, F32)]
    body = functools.partial(within_body, len(chunk), size, block)
    return kernel(body, [(array, pltpu.VMEM) for array in arrays], outputs)


def attend_body(earlier, size, query, within, carry, *refs):
    others = refs[:earlier]
    w_first, top_out, bottom_out, top_first, bottom_first = refs[earlier:]
    heads = carry.shape[0]
    half = query.shape[0] // 2
    for h in range(heads):
        cut = slice(h * size, (h + 1) * size)
        prior = carry[h]
        for other in others:
            prior = prior + other[h].astype(F32)
        high = prior.astype(BF16)
        low = (prior - high.astype(F32)).astype(BF16)
        q = query[:, cut]
        o = within[:, cut] + dot(jnp.concatenate([q, q], 1), jnp.concatenate([high, low], 0))
        o = o * lax.rsqrt(jnp.mean(o * o, axis=-1, keepdims=True) + EPSILON)
        attended = o.astype(BF16)
        top_out[:, cut] = attended[:half]
        bottom_out[:, cut] = attended[half:]
    block = 256 if w_first.shape[1] % 256 == 0 else 128

    for j in range(w_first.shape[1] // block):
        cut = slice(j * block, (j + 1) * block)
        weight = w_first[:, cut]
        top_first[:, cut] = dot(top_out[...], weight).astype(BF16)
        bottom_first[:, cut] = dot(bottom_out[...], weight).astype(BF16)


def attend(query, within, carry, others, w_first, size):
    rows, width = query.shape
    inputs = [(s, pltpu.VMEM) for s in (query, within, carry, *others, w_first)]
    outputs = [((rows // 2, width), BF16)] * 2 + [((rows // 2, w_first.shape[1]), BF16)] * 2
    return kernel(functools.partial(attend_body, len(others), size), inputs, outputs)


def share_body(odd, own, *refs):
    *others, out = refs
    total = jnp.where(odd[0] == 1, 0.0, own[...])
    for other in others:
        total = total + other[...].astype(F32)
    out[...] = total.astype(BF16)


def finish_body(top_sum, bottom_sum, top, bottom, out, staged, moved):
    half, parts = top.shape[0], moved.shape[1]
    rows = half // parts
    copies = []
    for i, (total, last) in enumerate(((top_sum, top), (bottom_sum, bottom))):
        for p in range(parts):
            mine = slice(p * rows, (p + 1) * rows)
            cut = slice(i * half + p * rows, i * half + (p + 1) * rows)
            staged[cut] = (total[mine] + last[mine].astype(F32)).astype(BF16)
            copies.append(pltpu.make_async_copy(staged.at[cut, :], out.at[cut, :], moved.at[i, p]))
            copies[-1].start()
    for copy in copies:
        copy.wait()


def finish(arrays):
    shape = (2 * arrays[0].shape[0], arrays[0].shape[1])
    return pl.pallas_call(
        finish_body,
        in_specs=[pl.BlockSpec(memory_space=pltpu.VMEM)] * 4,
        out_specs=pl.BlockSpec(memory_space=pltpu.HBM),
        out_shape=jax.ShapeDtypeStruct(shape, BF16),
        scratch_shapes=[pltpu.VMEM(shape, BF16), pltpu.SemaphoreType.DMA((2, 4))],
        compiler_params=pltpu.CompilerParams(vmem_limit_bytes=16 << 20),
        cost_estimate=pl.CostEstimate(flops=0, bytes_accessed=1 << 20, transcendentals=0),
    )(*arrays)


def local(tokens, w_query, w_key, w_value, w_out, carry):
    row_count = tokens.shape[0]
    head_count, size = carry.shape[:2]
    block = size * (2 if head_count % 2 == 0 else 1)
    half = row_count // 2
    count = lax.axis_size("tp")
    reach = count // 2
    order = ring_order(count)[::-1]
    forward = [(order[i], order[(i + 1) % count]) for i in range(count)]
    backward = [(b, a) for a, b in forward]
    index = lax.axis_index("tp")
    depth = tokens.shape[1]
    columns = w_out.shape[1] // count

    offsets = list(range(-reach + 1, reach + 1))
    numbers = [
        lookup([order[(order.index(i) + offset) % count] for i in range(count)], index)
        for offset in offsets
    ]
    column_starts = [n * columns for n in numbers]
    row_table = jnp.stack([n * depth for n in numbers])
    column_table = jnp.stack(column_starts)
    odd = jnp.reshape(lax.rem(lax.axis_index("seq"), 2), (1,))
    tokens, odd, row_table, column_table, column_starts = lax.optimization_barrier(
        (tokens, odd, row_table, column_table, column_starts)
    )

    def add(item, chunk, held, sums):
        bring = [i for i in ((1, 2) if item == 0 else (item + 2,)) if i < len(offset_of)]
        bring = [offsets.index(offset_of[i]) for i in bring]
        extra = None
        if item == len(offset_of) - 2:
            bring, extra = [offsets.index(reach)], (w_out, column_table, columns)
        now, held = (held[0], held[1:]) if held else (None, [])
        place = offsets.index(offset_of[item])
        sums, sets, rest = project(
            chunk, row_table, place, weights, now, sums, block, bring, extra
        )
        held = [*held, *sets, *rest]
        return sums, held

    weights = (w_query, w_key, w_value)
    offset_of = [0]
    for step in range(1, reach):
        offset_of += [-step, step]
    windows = 2 * reach - 1
    ahead = {(0, 0): tokens[:half], (0, 1): tokens[half:]}
    behind = dict(ahead)

    def send(slot):
        level, second = divmod(slot - 1, 2)
        up, down = (level, second), (level, 1 - second)
        ahead[level + 1, second] = lax.ppermute(ahead[up], "tp", forward)
        behind[level + 1, 1 - second] = lax.ppermute(behind[down], "tp", backward)

    def halves(offset):
        side = ahead if offset < 0 else behind
        return [side[abs(offset), 0], side[abs(offset), 1]]

    send(1)
    send(2)
    sums, held = add(0, halves(0), [], None)
    for window in range(2, windows):
        level, second = divmod(window, 2)
        up, down = (level, second), (level, 1 - second)
        ahead[up], behind[down], sums, held = lax.optimization_barrier(
            (ahead[up], behind[down], sums, held)
        )
        send(window + 1)
        if window > 2:
            sums, held = add(window - 2, halves(offset_of[window - 2]), held, sums)
    up, down = (reach - 1, 1), (reach - 1, 0)
    ahead[up], behind[down], sums, held = lax.optimization_barrier(
        (ahead[up], behind[down], sums, held)
    )
    for item in (windows - 2, windows - 1):
        sums, held = add(item, halves(offset_of[item]), held, sums)
    final = [*held[0], held[1]]
    ahead, behind = ahead[reach, 0], behind[reach, 1]
    last = [ahead, behind]
    w_query_last, w_key_last, w_value_last, w_first = final
    keys, values = [None, None], [None, None]
    key_arrays = (w_key_last, w_value_last, sums[1], sums[2])
    keys[0], values[0], state = finish_keys(last[0], 0, *key_arrays, None, block, size)
    keys[1], values[1], state, sent = finish_keys(last[1], 1, *key_arrays, state, block, size)

    members = lax.axis_size("seq")
    others = [
        lax.ppermute(sent, "seq", [(i, i + shift) for i in range(members - shift)])
        for shift in range(2, members, 2)
    ]
    query, within = finish_query(last, w_query_last, sums[0], keys, values, block, size)
    others, query, within = lax.optimization_barrier((others, query, within))
    share = kernel(
        share_body,
        [(odd, pltpu.SMEM), (state, pltpu.VMEM), *[(other, pltpu.VMEM) for other in others]],
        [(state.shape, BF16)],
    )[0]
    others.append(lax.ppermute(share, "seq", [(i, i ^ 1) for i in range(members)]))

    *parts, top, bottom = attend(query, within, carry, others, w_first, size)

    def partial(rows, offset):
        start = column_starts[offsets.index(offset)]
        return dot(parts[rows], cut_at(w_out, start, columns, 1))

    up = [lax.ppermute(top, "tp", forward), None]
    down = [None, lax.ppermute(bottom, "tp", backward)]
    for distance in range(reach - 1, 0, -1):
        for rows in (0, 1):
            for held, sign, hops in ((up, 1, forward), (down, -1, backward)):
                value = partial(rows, sign * distance)
                if held[rows] is not None:
                    value = value + held[rows].astype(F32)
                held[rows] = lax.ppermute(value.astype(BF16), "tp", hops)
    top_sum = partial(0, 0) + down[0].astype(F32)
    bottom_sum = partial(1, 0) + up[1].astype(F32)
    return finish((top_sum, bottom_sum, up[0], down[1]))


def solution(mesh):
    placed = (
        P("seq", "tp"),
        P(None, "tp"),
        P(None, "tp"),
        P(None, "tp"),
        P("tp", None),
        P("tp", None, None),
    )
    return jax.shard_map(
        local, mesh=mesh, in_specs=placed, out_specs=P("seq", "tp"), check_vma=False
    )
```
